128 devices in a mesh: group: 16 (over x, z), local: 8 (over y, core).
Axes of the slice: x: 4, y: 4, z: 4, core: 2. Of those that a mesh axis runs over, the one named last changes fastest.
Arguments:
- states_in: bfloat16 [128, 7168], P(('group', 'local')), may hold values from -24 to 24
- queries: bfloat16 [128, 128, 576], P(('group', 'local')), may hold values from -320 to 320
- kv_cache: bfloat16 [128, 1024, 576], P(('group', 'local')), may hold values from -5 to 5
- kv_new: bfloat16 [128, 576], P(('group', 'local')), may hold values from -12 to 12
- lengths: int32 [128], P(('group', 'local')), may hold values from 2 to 1024, as said below
- w_uv: bfloat16 [128, 512, 128], P(('group', 'local')), may hold values from -1.5 to 1.5
- w_out: bfloat16 [16384, 7168], P(('group', 'local')), may hold values from -0.046875 to 0.046875
- norm_gain: float32 [7168], replicated, may hold values from 0.25 to 1.75
- expert_ids: int32 [128, 8], P(('group', 'local')), may hold values from 0 to 47, as said below
- route_scores: float32 [128, 8], P(('group', 'local')), may hold values from 0.05 to 1
- w_gate: bfloat16 [48, 7168, 1024], P('group', None, 'local'), may hold values from -0.0625 to 0.0625
- w_up: bfloat16 [48, 7168, 1024], P('group', None, 'local'), may hold values from -0.0625 to 0.0625
- w_down: bfloat16 [48, 1024, 7168], P('group', 'local'), may hold values from -0.1875 to 0.1875
Outputs:
- residual: bfloat16 [128, 7168], P(('group', 'local'))
- layer_out: bfloat16 [128, 7168], P(('group', 'local'))
The draws below stay inside these ranges and needn't reach their ends.
Inputs may be any that keep to these rules, and one draw needn't show every extreme that they name: Each request attends to the first lengths entries of its cache and to its new token; some request has all 1024. `expert_ids`: each row names 8 different experts, all within at most 4 groups, where group g holds experts g * 6 to g * 6 + 5.
All inputs are finite; a program needn't handle non-finite values.
Results may differ from the reference program's by a relative error of at most 0.015.
Values may be sent and summed in bfloat16 or wider, within the bound.
No kernel may reach another device: no remote copies, remote signals or barrier semaphores. Data moves between devices by JAX's collectives and lax.ppermute only.
A program may use at most 128 MiB of HBM per device.

```python
import math
import jax
import jax.numpy as jnp
from jax import lax

D = 7168
HEADS = 128
LAT = 512
ROPE = 64
VD = 128
EH = 1024
NGRP = 8
EXP_DEV = 3
TOPK = 8
TOPG = 4
CACHE = 1024
ROWS = 128
EXPERTS = 48
EXP_GRP = 6


def draw_kv_cache(key, part):
    own_key = jax.random.fold_in(key, 11)
    values = jnp.clip(jax.random.normal(own_key, (ROWS, CACHE, LAT + ROPE), jnp.float32), -5.0, 5.0)
    return values.astype(jnp.bfloat16)


def draw_queries(key, part):
    own_key = jax.random.fold_in(key, 13)
    values = jnp.clip(jax.random.normal(own_key, (ROWS, HEADS, LAT + ROPE), jnp.float32), -5.0, 5.0)
    return values.astype(jnp.bfloat16)


def draw_states_in(key, part):
    first_key, second_key, third_key = jax.random.split(key, 3)
    row_scale = jnp.exp(jax.random.uniform(second_key, (ROWS, 1), jnp.float32, math.log(0.4), math.log(2.5)))
    column_scale = jnp.exp(jax.random.uniform(third_key, (1, D), jnp.float32, math.log(0.3), math.log(3.0)))
    values = jnp.clip(jax.random.normal(first_key, (ROWS, D), jnp.float32), -4.0, 4.0) * row_scale * column_scale
    return jnp.clip(values, -24.0, 24.0).astype(jnp.bfloat16)


def draw_lengths(key, part):
    first_key, second_key, third_key = jax.random.split(key, 3)
    halvings = jax.random.randint(first_key, (ROWS,), 0, 4)
    longest = jnp.right_shift(jnp.full((ROWS,), CACHE, jnp.int32), halvings)
    trimmed = longest - jax.random.randint(second_key, (ROWS,), 0, CACHE // 16 + 1)
    chosen_row = jax.random.randint(third_key, (), 0, ROWS)
    return jnp.where(jnp.arange(ROWS) == chosen_row, CACHE, jnp.maximum(trimmed, 2)).astype(jnp.int32)


def draw_expert_ids(key, part):
    first_key, second_key, third_key = jax.random.split(key, 3)
    group_total = NGRP
    favour = jax.random.randint(first_key, (group_total,), 0, 3) * 131072
    group_score = (jax.random.randint(second_key, (ROWS, group_total), 0, 262144) + favour[None, :]) * 64 + jnp.arange(group_total, dtype=jnp.int32)[None, :]
    ignored, groups = lax.top_k(group_score, TOPG)
    candidates = TOPG * EXP_GRP
    pick_score = jax.random.randint(third_key, (ROWS, candidates), 0, 262144) * 1024 + jnp.arange(candidates, dtype=jnp.int32)[None, :]
    ignored_too, picks = lax.top_k(pick_score, TOPK)
    group_of = jnp.take_along_axis(groups, picks // EXP_GRP, axis=1)
    return (group_of * EXP_GRP + picks % EXP_GRP).astype(jnp.int32)


def level_of(stream_key, extent, cuts, smallest, high):
    factor_of = 1.0
    for axis_at, shards_of in cuts:
        heights = jax.random.uniform(jax.random.fold_in(jax.random.fold_in(stream_key, 6), axis_at), (shards_of,), jnp.float32, smallest / len(cuts), high / len(cuts))
        factor_of = factor_of * jnp.repeat(jnp.exp(heights), extent[axis_at] // shards_of).reshape((-1,) + (1,) * (len(extent) - 1 - axis_at))
    return factor_of


def noise(key, dims, width, limit, cuts=(), kind=jnp.bfloat16):
    gain = level_of(key, dims, cuts, -0.22, 0.18) if cuts else 1.0
    result = jax.random.normal(key, dims, jnp.float32) * width * gain
    return jnp.minimum(jnp.maximum(result, -limit), limit).astype(kind)


def setup_inputs(seed: int = 0) -> dict:
    key_of = jax.random.split(jax.random.key(seed), 14)
    states_in = draw_states_in(jax.random.fold_in(key_of[13], 71), 0)
    queries = draw_queries(jax.random.fold_in(key_of[13], 71), 0)
    kv_cache = draw_kv_cache(jax.random.fold_in(key_of[13], 71), 0)
    kv_new = noise(key_of[3], (ROWS, LAT + ROPE), 2.0, 12.0, ((0, 128),))
    lengths = draw_lengths(jax.random.fold_in(key_of[13], 71), 0)
    w_uv = noise(key_of[5], (HEADS, LAT, VD), 0.25, 1.5, ((0, 128),))
    w_out = noise(key_of[6], (HEADS * VD, D), (HEADS * VD) ** -0.5, 0.046875, ((0, 128),))
    norm_gain = jnp.clip(1.0 + 0.15 * jax.random.normal(key_of[7], (D,), jnp.float32), 0.25, 1.75)
    expert_ids = draw_expert_ids(jax.random.fold_in(key_of[13], 71), 0)
    route_scores = jnp.clip(jnp.exp(math.log(1.0) - 2.9957323 * jax.random.uniform(key_of[9], (ROWS, TOPK), jnp.float32) ** level_of(key_of[9], (ROWS, TOPK), ((0, 128),), -0.2, 0.2)), 0.05, 1.0)
    w_gate = noise(key_of[10], (EXPERTS, D, EH), D ** -0.5, 0.0625, ((0, 16), (2, 8)))
    w_up = noise(key_of[11], (EXPERTS, D, EH), D ** -0.5, 0.0625, ((0, 16), (2, 8)))
    w_down = noise(key_of[12], (EXPERTS, EH, D), EH ** -0.5, 0.1875, ((0, 16), (1, 8)))
    return {"states_in": states_in, "queries": queries, "kv_cache": kv_cache, "kv_new": kv_new, "lengths": lengths, "w_uv": w_uv, "w_out": w_out, "norm_gain": norm_gain, "expert_ids": expert_ids, "route_scores": route_scores, "w_gate": w_gate, "w_up": w_up, "w_down": w_down}


def attend_one(packed):
    query, cache_rows, newest, length = packed
    softmax_scale = (VD + ROPE) ** (-0.5)
    cached = jnp.dot(query, cache_rows.T, preferred_element_type=jnp.float32) * softmax_scale
    own_score = jnp.dot(query, newest, preferred_element_type=jnp.float32) * softmax_scale
    visible = (jnp.arange(CACHE, dtype=jnp.int32) < length)[None, :]
    highest = jnp.maximum(lax.optimization_barrier(jnp.max(jnp.where(visible, cached, -1e+30), axis=1)), own_score)
    weights_cached = jnp.exp(jnp.where(visible, cached - highest[:, None], -1e+30))
    weight_own = jnp.exp(own_score - highest)
    denominator = lax.optimization_barrier(jnp.sum(weights_cached, axis=1)) + weight_own
    probs_cached = (weights_cached / denominator[:, None]).astype(jnp.bfloat16)
    prob_own = (weight_own / denominator).astype(jnp.bfloat16)
    blended = jnp.dot(probs_cached, cache_rows[:, :LAT], preferred_element_type=jnp.float32)
    blended = blended + prob_own.astype(jnp.float32)[:, None] * newest[:LAT].astype(jnp.float32)[None, :]
    return blended.astype(jnp.bfloat16)

def reference(states_in, queries, kv_cache, kv_new, lengths, w_uv, w_out, norm_gain, expert_ids, route_scores, w_gate, w_up, w_down):
    latent_out = lax.map(attend_one, (queries, kv_cache, kv_new, lengths))
    values = jnp.einsum('rhl,hlv->rhv', latent_out.astype(jnp.float32), w_uv.astype(jnp.float32)).astype(jnp.bfloat16)
    attention = jnp.dot(values.reshape(ROWS, HEADS * VD), w_out, preferred_element_type=jnp.float32)
    residual = (states_in.astype(jnp.float32) + attention).astype(jnp.bfloat16)
    widened = residual.astype(jnp.float32)
    normed = (widened * lax.rsqrt(lax.optimization_barrier(jnp.mean(widened * widened, axis=1, keepdims=True)) + 1e-06) * norm_gain).astype(jnp.bfloat16)
    route_weights = (2.5 * route_scores / lax.optimization_barrier(jnp.sum(route_scores, axis=1, keepdims=True))).astype(jnp.bfloat16)
    chosen = expert_ids[:, :, None] == jnp.arange(EXPERTS, dtype=jnp.int32)[None, None, :]
    dense_weights = lax.optimization_barrier(jnp.sum(jnp.where(chosen, route_weights.astype(jnp.float32)[:, :, None], jnp.float32(0.0)), axis=1))
    block_total = EXPERTS // EXP_DEV
    by_block = dense_weights.reshape(ROWS, block_total, EXP_DEV)

    def one_block(carried, packed):
        index, gate_rows, up_rows, down_rows = packed
        weights = lax.dynamic_index_in_dim(by_block, index, axis=1, keepdims=False)
        part_sum = jnp.zeros((ROWS, D), jnp.float32)
        for expert in range(EXP_DEV):
            gate_proj = jnp.dot(normed, gate_rows[expert], preferred_element_type=jnp.float32)
            up_proj = jnp.dot(normed, up_rows[expert], preferred_element_type=jnp.float32)
            active = (jax.nn.silu(gate_proj) * up_proj).astype(jnp.bfloat16)
            output = jnp.dot(active, down_rows[expert], preferred_element_type=jnp.float32)
            part_sum = part_sum + weights[:, expert:expert + 1] * output
        rounded = lax.optimization_barrier(part_sum.astype(jnp.bfloat16))
        return (carried + rounded.astype(jnp.float32), None)
    indices = jnp.arange(block_total, dtype=jnp.int32)
    start_sum = jnp.zeros((ROWS, D), jnp.float32)
    expert_sum, unused = lax.scan(one_block, start_sum, (indices, w_gate.reshape(block_total, EXP_DEV, D, EH), w_up.reshape(block_total, EXP_DEV, D, EH), w_down.reshape(block_total, EXP_DEV, EH, D)))
    layer_out = (residual.astype(jnp.float32) + expert_sum).astype(jnp.bfloat16)
    return (residual, layer_out)
```

```python
import jax
import jax.numpy as jnp
from jax import lax
from jax.experimental import pallas as pl
from jax.experimental.pallas import tpu as pltpu
from jax.sharding import Mesh, PartitionSpec as P

LAT = 512
ROPE = 64
VD = 128
NX, NZ, NY = 4, 4, 4
CHIPS = NX * NZ * NY
GROUPS = NX * NZ
CHIP_AXES = ("x", "z", "y")
ALL_AXES = ("x", "z", "y", "core")
SWAP = [(0, 1), (1, 0)]
BF = jnp.bfloat16
F32 = jnp.float32


def swap(value):
    return lax.ppermute(value, "core", SWAP)


def exchange(value):
    return lax.all_to_all(value, CHIP_AXES, split_axis=0, concat_axis=0, tiled=True)


def interleave(core, own, other):
    first = jnp.where(core == 0, own, other)
    second = jnp.where(core == 0, other, own)
    return jnp.stack([first, second], axis=1).reshape((-1,) + own.shape[1:])


def out_kernel(core_ref, values_ref, own_ref, other_ref, out_ref):
    del core_ref
    weights = jnp.concatenate([own_ref[...], other_ref[...]], axis=0)
    product = jnp.dot(values_ref[...], weights, preferred_element_type=F32)
    out_ref[...] = product.astype(BF).reshape(out_ref.shape)


def out_projection(core, values, own, other):
    rows = values.shape[0]
    wide = own.shape[1] // 8
    spec = pl.BlockSpec((own.shape[0], wide), lambda y, c: (0, 4 * c[0] + y))
    return pl.pallas_call(
        out_kernel,
        grid_spec=pltpu.PrefetchScalarGridSpec(
            num_scalar_prefetch=1,
            grid=(NY,),
            in_specs=[pl.BlockSpec(values.shape, lambda y, c: (0, 0)), spec, spec],
            out_specs=pl.BlockSpec((rows // 8, 1, 8, wide), lambda y, c: (0, y, 0, 0)),
        ),
        out_shape=jax.ShapeDtypeStruct((rows // 8, NY, 8, wide), BF),
        name="out_projection",
    )(core[None], values, own, other)


def gate_up_kernel(
    core_ref, own_ref, other_ref, gain_ref, route_ref, gate_ref, up_ref, act_ref, inverse_ref, sum_ref
):
    del core_ref
    step = pl.program_id(0)
    rows = act_ref.shape[0]
    wide = own_ref.shape[-1]
    experts = gate_ref.shape[0]

    def part(ref, y):
        return ref[:, y].reshape(rows, wide)

    @pl.when(step == 0)
    def _():
        total = jnp.zeros((rows, 1), F32)
        for ref in (own_ref, other_ref):
            for y in range(NY):
                piece = part(ref, y).astype(F32)
                total = total + jnp.sum(piece * piece, axis=1, keepdims=True)
        inverse_ref[...] = lax.rsqrt(total / (8 * wide) + 1e-06)
        sum_ref[...] = jnp.zeros_like(sum_ref)

    def accumulate(ref, y):
        piece = jnp.concatenate([part(ref, y), part(ref, y + 1)], axis=1).astype(F32)
        normed = (piece * inverse_ref[...] * gain_ref[...]).astype(BF)
        for e in range(experts):
            weights = jnp.concatenate([gate_ref[e], up_ref[e]], axis=1)
            sum_ref[e] += jnp.dot(normed, weights, preferred_element_type=F32)

    for index, (ref, y) in enumerate(((own_ref, 0), (own_ref, 2), (other_ref, 0), (other_ref, 2))):
        pl.when(step == index)(lambda ref=ref, y=y: accumulate(ref, y))

    @pl.when(step == 3)
    def _():
        for e in range(experts):
            hidden = act_ref.shape[1] // experts
            gate = sum_ref[e, :, :hidden]
            up = sum_ref[e, :, hidden:]
            active = gate / (1.0 + jnp.exp(-gate)) * up
            active = active * route_ref[:, e : e + 1].astype(F32)
            act_ref[:, e * hidden : (e + 1) * hidden] = active.astype(BF)


def gate_up(core, own, other, gain, route, w_gate, w_up):
    groups, _, eight, wide = own.shape
    rows = groups * eight
    experts, model, hidden = w_gate.shape

    def block(step, c):
        half = jnp.where(step < 2, c[0], 1 - c[0])
        return 2 * half + step % 2

    weights = pl.BlockSpec((experts, 2 * wide, hidden), lambda s, c: (0, block(s, c), 0))
    whole = pl.BlockSpec(own.shape, lambda s, c: (0, 0, 0, 0))
    return pl.pallas_call(
        gate_up_kernel,
        grid_spec=pltpu.PrefetchScalarGridSpec(
            num_scalar_prefetch=1,
            grid=(4,),
            in_specs=[
                whole,
                whole,
                pl.BlockSpec((1, 2 * wide), lambda s, c: (0, block(s, c))),
                pl.BlockSpec(route.shape, lambda s, c: (0, 0)),
                weights,
                weights,
            ],
            out_specs=pl.BlockSpec((rows, experts * hidden), lambda s, c: (0, 0)),
            scratch_shapes=[
                pltpu.VMEM((rows, 1), F32),
                pltpu.VMEM((experts, rows, 2 * hidden), F32),
            ],
        ),
        out_shape=jax.ShapeDtypeStruct((rows, experts * hidden), BF),
        name="gate_up",
    )(core[None], own, other, gain[None], route, w_gate, w_up)


def down_kernel(core_ref, act_own_ref, act_other_ref, own_ref, other_ref, out_ref):
    del core_ref
    act = jnp.concatenate([act_own_ref[...], act_other_ref[...]], axis=1)
    weights = jnp.concatenate([own_ref[...], other_ref[...]], axis=0)
    out_ref[...] = jnp.dot(act, weights, preferred_element_type=F32).astype(BF)


def down(core, act_own, act_other, own, other):
    rows = act_own.shape[0]
    wide = own.shape[1] // 8
    act = pl.BlockSpec(act_own.shape, lambda y, c: (0, 0))
    spec = pl.BlockSpec((own.shape[0], wide), lambda y, c: (0, 4 * c[0] + y))
    return pl.pallas_call(
        down_kernel,
        grid_spec=pltpu.PrefetchScalarGridSpec(
            num_scalar_prefetch=1,
            grid=(NY,),
            in_specs=[act, act, spec, spec],
            out_specs=pl.BlockSpec((rows, wide), lambda y, c: (0, y)),
        ),
        out_shape=jax.ShapeDtypeStruct((rows, NY * wide), BF),
        name="down",
    )(core[None], act_own, act_other, own, other)


def attend(queries, kv_cache, kv_new, lengths):
    cache_len = kv_cache.shape[1]
    requests = queries.shape[0]
    softmax_scale = (VD + ROPE) ** (-0.5)
    cached = (
        jnp.einsum("rhc,rkc->rhk", queries, kv_cache, preferred_element_type=F32) * softmax_scale
    )
    own_score = jnp.einsum("rhc,rc->rh", queries, kv_new, preferred_element_type=F32) * softmax_scale
    visible = lax.broadcasted_iota(jnp.int32, (requests, 1, cache_len), 2) < lengths[:, None, None]
    highest = jnp.maximum(jnp.max(jnp.where(visible, cached, -1e30), axis=2), own_score)
    weights_cached = jnp.exp(jnp.where(visible, cached - highest[:, :, None], -1e30))
    weight_own = jnp.exp(own_score - highest)
    denominator = jnp.sum(weights_cached, axis=2) + weight_own
    probs_cached = (weights_cached / denominator[:, :, None]).astype(BF)
    prob_own = (weight_own / denominator).astype(BF)
    blended = jnp.einsum(
        "rhk,rkl->rhl", probs_cached, kv_cache[:, :, :LAT], preferred_element_type=F32
    )
    blended = blended + prob_own.astype(F32)[:, :, None] * kv_new[:, None, :LAT].astype(F32)
    return blended.astype(BF)


def body(
    states_in,
    queries,
    kv_cache,
    kv_new,
    lengths,
    w_uv,
    w_out,
    norm_gain,
    expert_ids,
    route_scores,
    w_gate,
    w_up,
    w_down,
):
    core = lax.axis_index("core")
    group = lax.axis_index("x") * NZ + lax.axis_index("z")
    y_at = lax.axis_index("y")
    model = states_in.shape[1]
    half = model // 2
    wide = half // NY
    experts = w_gate.shape[0]
    expert_total = experts * GROUPS
    down_own = w_down.reshape(-1, model)
    uv_other = swap(w_uv)
    out_other = swap(w_out)
    down_other = swap(down_own)
    states_swapped = swap(states_in)

    latent_out = attend(queries, kv_cache, kv_new, lengths)[0]

    route_weights = (2.5 * route_scores / jnp.sum(route_scores, axis=1, keepdims=True)).astype(BF)
    chosen = expert_ids[:, :, None] == lax.broadcasted_iota(jnp.int32, (1, 1, expert_total), 2)
    dense_weights = jnp.sum(jnp.where(chosen, route_weights.astype(F32)[:, :, None], 0.0), axis=1)
    by_block = dense_weights.reshape(GROUPS, 1, 1, experts).astype(BF)
    by_block = jnp.broadcast_to(
        jnp.pad(by_block, ((0, 0), (0, 0), (0, 0), (0, 128 - experts))), (GROUPS, NY, 2, 128)
    ).reshape(CHIPS, 2, 128)

    own_half = lax.dynamic_slice_in_dim(states_in, core * half, half, 1)
    other_half = lax.dynamic_slice_in_dim(states_swapped, core * half, half, 1)
    chip_states = interleave(core, own_half, other_half)
    chip_states = chip_states.reshape(2, NY, wide).transpose(1, 0, 2)
    chip_states = jnp.broadcast_to(chip_states[None], (GROUPS, NY, 2, wide)).reshape(CHIPS, 2, wide)

    sent = jnp.concatenate([latent_out.reshape(CHIPS, 2, LAT), by_block, chip_states], axis=2)
    got = exchange(sent)

    latent_own = lax.dynamic_index_in_dim(got, core, 1, keepdims=False)[:, :LAT]
    latent_other = lax.dynamic_index_in_dim(got, 1 - core, 1, keepdims=False)[:, :LAT]
    route_rows = got[:, 0, LAT : LAT + 128]
    my_states = lax.dynamic_slice_in_dim(got[:, :, LAT + 128 :], group * NY, NY, 0).reshape(8, wide)

    value_own = jnp.dot(latent_own, w_uv[0], preferred_element_type=F32).astype(BF)
    value_other = jnp.dot(latent_other, uv_other[0], preferred_element_type=F32).astype(BF)
    mine = jnp.concatenate([value_own, value_other, route_rows], axis=1)
    theirs_sent = jnp.concatenate([value_other, value_own, route_rows], axis=1)
    rows_all = interleave(core, mine, swap(theirs_sent))
    values = rows_all[:, : 2 * VD]
    route = rows_all[:, 2 * VD :]

    partial = out_projection(core, values, w_out, out_other)
    partial = exchange(partial.reshape(CHIPS, 8, wide))
    attention = jnp.sum(partial.astype(F32), axis=0)
    residual_part = (my_states.astype(F32) + attention).astype(BF)
    rows_own = exchange(jnp.broadcast_to(residual_part[None], (CHIPS, 8, wide)))
    rows_other = swap(rows_own)
    rows_own = rows_own.reshape(GROUPS, NY, 8, wide)
    rows_other = rows_other.reshape(GROUPS, NY, 8, wide)

    act = gate_up(core, rows_own, rows_other, norm_gain, route, w_gate, w_up)
    act_other = swap(act)
    output = down(core, act, act_other, down_own, down_other)
    output = output.reshape(CHIPS, 2, half // 128, 128).transpose(0, 2, 1, 3)
    output = exchange(output.reshape(CHIPS, half // 64, 128))
    expert_sum = jnp.sum(output.astype(F32), axis=0)
    expert_sum = expert_sum.reshape(half // 128, 2, 128).transpose(1, 0, 2).reshape(2, half)

    def chip_rows(rows):
        mine = lax.dynamic_index_in_dim(rows, group, 0, keepdims=False)
        mine = lax.dynamic_slice_in_dim(mine, 2 * y_at, 2, 1)
        return mine.transpose(1, 0, 2).reshape(2, half)

    residual_own = chip_rows(rows_own)
    residual_other = chip_rows(rows_other)
    layer_half = (residual_own.astype(F32) + expert_sum).astype(BF)
    layer_mine = lax.dynamic_slice_in_dim(layer_half, core, 1, 0)
    layer_got = swap(lax.dynamic_slice_in_dim(layer_half, 1 - core, 1, 0))
    residual_mine = lax.dynamic_slice_in_dim(residual_own, core, 1, 0)
    residual_got = lax.dynamic_slice_in_dim(residual_other, core, 1, 0)

    def joined(mine, got):
        return jnp.where(
            core == 0, jnp.concatenate([mine, got], axis=1), jnp.concatenate([got, mine], axis=1)
        )

    return (joined(residual_mine, residual_got), joined(layer_mine, layer_got))


def solution(mesh):
    fine = Mesh(mesh.devices.reshape(NX, NZ, NY, 2), ALL_AXES)
    rows = P(ALL_AXES, None)
    cube = P(ALL_AXES, None, None)
    in_specs = (
        rows,
        cube,
        cube,
        rows,
        P(ALL_AXES),
        cube,
        rows,
        P(),
        rows,
        rows,
        P(("x", "z"), None, ("y", "core")),
        P(("x", "z"), None, ("y", "core")),
        P(("x", "z"), ("y", "core"), None),
    )
    return jax.shard_map(body, mesh=fine, in_specs=in_specs, out_specs=(rows, rows), check_vma=False)
```

```python
import jax
import jax.numpy as jnp
from jax import lax
from jax.experimental import pallas as pl
from jax.experimental.pallas import tpu as pltpu
from jax.sharding import Mesh, PartitionSpec as P

LAT = 512
ROPE = 64
VD = 128
NX, NZ, NY = 4, 4, 4
CHIPS = NX * NZ * NY
GROUPS = NX * NZ
CHIP_AXES = ("x", "z", "y")
ALL_AXES = ("x", "z", "y", "core")
SWAP = [(0, 1), (1, 0)]
BF = jnp.bfloat16
F32 = jnp.float32


def swap(value):
    return lax.ppermute(value, "core", SWAP)


def exchange(value):
    return lax.all_to_all(value, CHIP_AXES, split_axis=0, concat_axis=0, tiled=True)


def limit(mib):
    return pltpu.CompilerParams(vmem_limit_bytes=mib * 1024 * 1024)


SENT_ROWS = 24
ROUTE_ROW = 8
STATE_ROW = 9


def attend_kernel(
    length_ref, query_ref, cache_ref, newest_ref, states_ref, ids_ref, score_ref, sent_ref, latent_ref, pack_ref
):
    heads = query_ref.shape[1]
    positions = cache_ref.shape[1]
    lanes = 128
    softmax_scale = (VD + ROPE) ** (-0.5)
    contract_first = (((0,), (0,)), ((), ()))
    query = query_ref[...]
    cached = lax.dot_general(query, cache_ref[...], contract_first, preferred_element_type=F32)
    cached = cached * softmax_scale
    newest = newest_ref[...]
    newest_rows = jnp.broadcast_to(newest, (8, newest.shape[1]))
    own_score = lax.dot_general(
        query, newest_rows, (((0,), (1,)), ((), ())), preferred_element_type=F32
    )[:, :1]
    own_score = own_score * softmax_scale
    visible = lax.broadcasted_iota(jnp.int32, (heads, positions), 1) < length_ref[0]
    cached = jnp.where(visible, cached, -1e30)
    highest = jnp.maximum(jnp.max(cached, axis=1, keepdims=True), own_score)
    weights = jnp.where(visible, jnp.exp(cached - highest), 0.0)
    weight_own = jnp.exp(own_score - highest)
    denominator = jnp.sum(weights, axis=1, keepdims=True) + weight_own
    probs = (weights / denominator).astype(BF)
    prob_own = (weight_own / denominator).astype(BF).astype(F32)
    blended = lax.dot_general(
        probs, cache_ref[:LAT, :], (((1,), (1,)), ((), ())), preferred_element_type=F32
    )
    blended = blended + prob_own * newest[:, :LAT].astype(F32)
    for t in range(LAT // lanes):
        latent_ref[t] = blended[:, t * lanes : (t + 1) * lanes]

    pieces = states_ref[...].astype(F32)
    half = pieces.shape[1] // 2
    wide = half // NY
    tiles = wide // lanes
    for y in range(NY):
        for side in range(2):
            for t in range(tiles):
                at = side * half + y * wide + t * lanes
                row = y * SENT_ROWS + STATE_ROW + side * tiles + t
                pack_ref[row : row + 1, :] = pieces[:, at : at + lanes]
        pack_ref[(y + 1) * SENT_ROWS - 1 : (y + 1) * SENT_ROWS, :] = jnp.zeros((1, lanes), F32)
    first = pack_ref[: NY * SENT_ROWS, :]
    for g in range(1, GROUPS):
        pack_ref[g * NY * SENT_ROWS : (g + 1) * NY * SENT_ROWS, :] = first

    scores = score_ref[...]
    routes = (2.5 * scores / jnp.sum(scores, axis=1, keepdims=True)).astype(BF).astype(F32)
    ids = ids_ref[...]
    per_block = 3
    block = lax.broadcasted_iota(jnp.int32, (CHIPS, lanes), 0) // NY
    lane = lax.broadcasted_iota(jnp.int32, (CHIPS, lanes), 1)
    expert = jnp.where(lane < per_block, block * per_block + lane, -1)
    dense = jnp.zeros((CHIPS, lanes), F32)
    for k in range(ids.shape[1]):
        dense = dense + jnp.where(expert == ids[:, k : k + 1], routes[:, k : k + 1], 0.0)
    pack_ref[pl.ds(ROUTE_ROW, CHIPS, stride=SENT_ROWS), :] = dense

    for t in range(LAT // lanes):
        for j in range(2):
            piece = latent_ref[t, pl.ds(j, CHIPS, stride=2), :]
            pack_ref[pl.ds(2 * t + j, CHIPS, stride=SENT_ROWS), :] = piece
    sent_ref[...] = pack_ref[...].astype(BF).reshape(sent_ref.shape)


def attend_and_pack(lengths, queries, kv_cache, kv_new, states_in, expert_ids, route_scores):
    whole = pl.BlockSpec(memory_space=pltpu.VMEM)
    return pl.pallas_call(
        attend_kernel,
        in_specs=[pl.BlockSpec(memory_space=pltpu.SMEM)] + [whole] * 6,
        out_specs=whole,
        out_shape=jax.ShapeDtypeStruct((CHIPS, SENT_ROWS, 128), BF),
        scratch_shapes=[
            pltpu.VMEM((LAT // 128, queries.shape[1], 128), F32),
            pltpu.VMEM((CHIPS * SENT_ROWS, 128), F32),
        ],
        compiler_params=limit(24),
        name="attend",
    )(lengths, queries[0].T, kv_cache[0].T, kv_new, states_in, expert_ids, route_scores)


VALUE_ROWS = 3 * CHIPS + 32


def value_kernel(place_ref, got_ref, own_ref, other_ref, mine_ref, send_ref, rows_ref, state_ref):
    core = place_ref[0]
    group = place_ref[1]
    lanes = 128
    rows_ref[...] = got_ref[...].astype(F32).reshape(rows_ref.shape)

    def latent(j):
        pieces = [
            rows_ref[pl.ds(2 * t + j, CHIPS, stride=SENT_ROWS), :].astype(BF) for t in range(LAT // lanes)
        ]
        return jnp.concatenate(pieces, axis=1)

    first, second = latent(0), latent(1)
    latent_own = jnp.where(core == 0, first, second)
    latent_other = jnp.where(core == 0, second, first)
    value_own = jnp.dot(latent_own, own_ref[...], preferred_element_type=F32).astype(BF)
    value_other = jnp.dot(latent_other, other_ref[...], preferred_element_type=F32).astype(BF)
    routes = rows_ref[pl.ds(ROUTE_ROW, CHIPS, stride=SENT_ROWS), :].astype(BF)
    base = pl.multiple_of(group * (NY * SENT_ROWS), 8)
    tiles = 7
    for side in range(2):
        state_ref[side] = jnp.zeros(state_ref.shape[1:], F32)
    for y in range(NY):
        source = rows_ref[pl.ds(base + y * SENT_ROWS, SENT_ROWS), :]
        for side in range(2):
            at = STATE_ROW + side * tiles
            state_ref[side, 8 * y : 8 * y + tiles, :] = source[at : at + tiles, :]
    low, high = state_ref[0], state_ref[1]
    for ref, a, b in ((mine_ref, value_own, value_other), (send_ref, value_other, value_own)):
        ref[:CHIPS, :] = a
        ref[CHIPS : 2 * CHIPS, :] = b
        ref[2 * CHIPS : 3 * CHIPS, :] = routes
    mine_ref[3 * CHIPS :, :] = jnp.where(core == 0, low, high).astype(BF)
    send_ref[3 * CHIPS :, :] = jnp.where(core == 0, high, low).astype(BF)


def project_values(place, got, own, other):
    whole = pl.BlockSpec(memory_space=pltpu.VMEM)
    out = jax.ShapeDtypeStruct((VALUE_ROWS, 128), BF)
    return pl.pallas_call(
        value_kernel,
        in_specs=[pl.BlockSpec(memory_space=pltpu.SMEM)] + [whole] * 3,
        out_specs=(whole, whole),
        out_shape=(out, out),
        scratch_shapes=[
            pltpu.VMEM((CHIPS * SENT_ROWS, 128), F32),
            pltpu.VMEM((2, 32, 128), F32),
        ],
        compiler_params=limit(16),
        name="values",
    )(place, got, own, other)


def out_kernel(
    place_ref, mine_ref, got_ref, own_ref, other_ref, out_ref, route_ref, states_ref, rows_ref, values_ref
):
    step = pl.program_id(0)
    core = place_ref[0]
    lanes = 128

    @pl.when(step == 0)
    def _():
        mine = mine_ref[...].astype(F32)
        got = got_ref[...].astype(F32)
        even = jnp.where(core == 0, mine, got)
        odd = jnp.where(core == 0, got, mine)
        for part in range(3):
            rows = slice(part * CHIPS, (part + 1) * CHIPS)
            rows_ref[pl.ds(0, CHIPS, stride=2), :] = even[rows]
            rows_ref[pl.ds(1, CHIPS, stride=2), :] = odd[rows]
            if part < 2:
                values_ref[:, part * lanes : (part + 1) * lanes] = rows_ref[...].astype(BF)
            else:
                route_ref[...] = rows_ref[...]
        tiles = states_ref.shape[1] // lanes
        for y in range(NY):
            for t in range(tiles):
                at = 3 * CHIPS + 8 * y + t
                cols = slice(t * lanes, (t + 1) * lanes)
                states_ref[2 * y : 2 * y + 1, cols] = even[at : at + 1, :]
                states_ref[2 * y + 1 : 2 * y + 2, cols] = odd[at : at + 1, :]

    weights = jnp.concatenate([own_ref[...], other_ref[...]], axis=0)
    product = jnp.dot(values_ref[...], weights, preferred_element_type=F32)
    out_ref[...] = product.astype(BF).reshape(out_ref.shape)


def out_projection(place, mine, got, own, other):
    rows = 2 * CHIPS
    wide = own.shape[1] // 8
    spec = pl.BlockSpec((own.shape[0], wide), lambda y, c: (0, 4 * c[0] + y))
    value = pl.BlockSpec(mine.shape, lambda y, c: (0, 0))
    return pl.pallas_call(
        out_kernel,
        grid_spec=pltpu.PrefetchScalarGridSpec(
            num_scalar_prefetch=1,
            grid=(NY,),
            in_specs=[value, value, spec, spec],
            out_specs=(
                pl.BlockSpec((rows // 8, 1, 8, wide), lambda y, c: (0, y, 0, 0)),
                pl.BlockSpec((rows, 128), lambda y, c: (0, 0)),
                pl.BlockSpec((8, wide), lambda y, c: (0, 0)),
            ),
            scratch_shapes=[pltpu.VMEM((rows, 128), F32), pltpu.VMEM((rows, 2 * VD), BF)],
        ),
        out_shape=(
            jax.ShapeDtypeStruct((rows // 8, NY, 8, wide), BF),
            jax.ShapeDtypeStruct((rows, 128), F32),
            jax.ShapeDtypeStruct((8, wide), F32),
        ),
        compiler_params=limit(16),
        name="out_projection",
    )(place, mine, got, own, other)


def gate_up_kernel(
    core_ref, own_ref, other_ref, gain_ref, route_ref, gate_ref, up_ref, act_ref, inverse_ref, sum_ref
):
    del core_ref
    step = pl.program_id(0)
    rows = act_ref.shape[0]
    wide = own_ref.shape[-1]
    experts = gate_ref.shape[0]

    def part(ref, y):
        return ref[:, y].reshape(rows, wide)

    @pl.when(step == 0)
    def _():
        total = jnp.zeros((rows, 1), F32)
        for ref in (own_ref, other_ref):
            for y in range(NY):
                piece = part(ref, y).astype(F32)
                total = total + jnp.sum(piece * piece, axis=1, keepdims=True)
        inverse_ref[...] = lax.rsqrt(total / (8 * wide) + 1e-06)
        sum_ref[...] = jnp.zeros_like(sum_ref)

    def accumulate(ref, y):
        piece = jnp.concatenate([part(ref, y), part(ref, y + 1)], axis=1).astype(F32)
        normed = (piece * inverse_ref[...] * gain_ref[...]).astype(BF)
        for e in range(experts):
            weights = jnp.concatenate([gate_ref[e], up_ref[e]], axis=1)
            sum_ref[e] += jnp.dot(normed, weights, preferred_element_type=F32)

    for index, (ref, y) in enumerate(((own_ref, 0), (own_ref, 2), (other_ref, 0), (other_ref, 2))):
        pl.when(step == index)(lambda ref=ref, y=y: accumulate(ref, y))

    @pl.when(step == 3)
    def _():
        for e in range(experts):
            hidden = act_ref.shape[1] // experts
            gate = sum_ref[e, :, :hidden]
            up = sum_ref[e, :, hidden:]
            active = gate / (1.0 + jnp.exp(-gate)) * up
            active = active * route_ref[:, e : e + 1]
            act_ref[:, e * hidden : (e + 1) * hidden] = active.astype(BF)


def gate_up(core, own, other, gain, route, w_gate, w_up):
    groups, _, eight, wide = own.shape
    rows = groups * eight
    experts, model, hidden = w_gate.shape

    def block(step, c):
        half = jnp.where(step < 2, c[0], 1 - c[0])
        return 2 * half + step % 2

    weights = pl.BlockSpec((experts, 2 * wide, hidden), lambda s, c: (0, block(s, c), 0))
    whole = pl.BlockSpec(own.shape, lambda s, c: (0, 0, 0, 0))
    return pl.pallas_call(
        gate_up_kernel,
        grid_spec=pltpu.PrefetchScalarGridSpec(
            num_scalar_prefetch=1,
            grid=(4,),
            in_specs=[
                whole,
                whole,
                pl.BlockSpec((1, 2 * wide), lambda s, c: (0, block(s, c))),
                pl.BlockSpec(route.shape, lambda s, c: (0, 0)),
                weights,
                weights,
            ],
            out_specs=pl.BlockSpec((rows, experts * hidden), lambda s, c: (0, 0)),
            scratch_shapes=[
                pltpu.VMEM((rows, 1), F32),
                pltpu.VMEM((experts, rows, 2 * hidden), F32),
            ],
        ),
        out_shape=jax.ShapeDtypeStruct((rows, experts * hidden), BF),
        compiler_params=limit(24),
        name="gate_up",
    )(core, own, other, gain[None], route, w_gate, w_up)


def down_kernel(core_ref, act_own_ref, act_other_ref, own_ref, other_ref, out_ref, sum_ref, pack_ref):
    del core_ref
    step = pl.program_id(0)
    lanes = 128
    stride = out_ref.shape[1]
    act = jnp.concatenate([act_own_ref[...], act_other_ref[...]], axis=1)
    weights = jnp.concatenate([own_ref[...], other_ref[...]], axis=0)
    product = jnp.dot(act, weights, preferred_element_type=F32)
    tiles = weights.shape[1] // lanes
    for t in range(tiles):
        sum_ref[t] = product[:, t * lanes : (t + 1) * lanes]

    def place(y):
        for t in range(tiles):
            for j in range(2):
                piece = sum_ref[t, pl.ds(j, CHIPS, stride=2), :]
                pack_ref[pl.ds(2 * (y * tiles + t) + j, CHIPS, stride=stride), :] = piece

    for index in range(NY):
        pl.when(step == index)(lambda index=index: place(index))

    @pl.when(step == NY - 1)
    def _():
        out_ref[...] = pack_ref[...].astype(BF).reshape(out_ref.shape)


def down(core, act_own, act_other, own, other):
    rows = act_own.shape[0]
    wide = own.shape[1] // 8
    out_rows = 2 * NY * wide // 128
    act = pl.BlockSpec(act_own.shape, lambda y, c: (0, 0))
    spec = pl.BlockSpec((own.shape[0], wide), lambda y, c: (0, 4 * c[0] + y))
    return pl.pallas_call(
        down_kernel,
        grid_spec=pltpu.PrefetchScalarGridSpec(
            num_scalar_prefetch=1,
            grid=(NY,),
            in_specs=[act, act, spec, spec],
            out_specs=pl.BlockSpec((CHIPS, out_rows, 128), lambda y, c: (0, 0, 0)),
            scratch_shapes=[
                pltpu.VMEM((wide // 128, rows, 128), F32),
                pltpu.VMEM((CHIPS * out_rows, 128), F32),
            ],
        ),
        out_shape=jax.ShapeDtypeStruct((CHIPS, out_rows, 128), BF),
        compiler_params=limit(20),
        name="down",
    )(core, act_own, act_other, own, other)


def body(
    states_in,
    queries,
    kv_cache,
    kv_new,
    lengths,
    w_uv,
    w_out,
    norm_gain,
    expert_ids,
    route_scores,
    w_gate,
    w_up,
    w_down,
):
    core = lax.axis_index("core")
    group = lax.axis_index("x") * NZ + lax.axis_index("z")
    y_at = lax.axis_index("y")
    model = states_in.shape[1]
    half = model // 2
    wide = half // NY
    down_own = w_down.reshape(-1, model)
    uv_other = swap(w_uv)
    out_other = swap(w_out)
    down_other = swap(down_own)
    place = jnp.stack([core, group])

    sent = attend_and_pack(
        lengths, queries, kv_cache, kv_new, states_in, expert_ids, route_scores
    )
    got = exchange(sent)
    mine, send = project_values(place, got, w_uv[0], uv_other[0])
    partial, route, my_states = out_projection(place, mine, swap(send), w_out, out_other)
    partial = exchange(partial.reshape(CHIPS, 8, wide))
    attention = jnp.sum(partial.astype(F32), axis=0)
    residual_part = (my_states + attention).astype(BF)
    rows_own = exchange(jnp.broadcast_to(residual_part[None], (CHIPS, 8, wide)))
    rows_other = swap(rows_own)
    rows_own = rows_own.reshape(GROUPS, NY, 8, wide)
    rows_other = rows_other.reshape(GROUPS, NY, 8, wide)

    act = gate_up(place, rows_own, rows_other, norm_gain, route, w_gate, w_up)
    act_other = swap(act)
    output = down(place, act, act_other, down_own, down_other)
    output = exchange(output)
    expert_sum = jnp.sum(output.astype(F32), axis=0)
    expert_sum = expert_sum.reshape(half // 128, 2, 128).transpose(1, 0, 2).reshape(2, half)

    def chip_rows(rows):
        mine = lax.dynamic_index_in_dim(rows, group, 0, keepdims=False)
        mine = lax.dynamic_slice_in_dim(mine, 2 * y_at, 2, 1)
        return mine.transpose(1, 0, 2).reshape(2, half)

    residual_own = chip_rows(rows_own)
    residual_other = chip_rows(rows_other)
    layer_half = (residual_own.astype(F32) + expert_sum).astype(BF)
    layer_mine = lax.dynamic_slice_in_dim(layer_half, core, 1, 0)
    layer_got = swap(lax.dynamic_slice_in_dim(layer_half, 1 - core, 1, 0))
    residual_mine = lax.dynamic_slice_in_dim(residual_own, core, 1, 0)
    residual_got = lax.dynamic_slice_in_dim(residual_other, core, 1, 0)

    def joined(mine, got):
        return jnp.where(
            core == 0, jnp.concatenate([mine, got], axis=1), jnp.concatenate([got, mine], axis=1)
        )

    return (joined(residual_mine, residual_got), joined(layer_mine, layer_got))


def solution(mesh):
    fine = Mesh(mesh.devices.reshape(NX, NZ, NY, 2), ALL_AXES)
    rows = P(ALL_AXES, None)
    cube = P(ALL_AXES, None, None)
    in_specs = (
        rows,
        cube,
        cube,
        rows,
        P(ALL_AXES),
        cube,
        rows,
        P(),
        rows,
        rows,
        P(("x", "z"), None, ("y", "core")),
        P(("x", "z"), None, ("y", "core")),
        P(("x", "z"), ("y", "core"), None),
    )
    return jax.shard_map(body, mesh=fine, in_specs=in_specs, out_specs=(rows, rows), check_vma=False)
```

```python
import jax
import jax.numpy as jnp
from jax import lax
from jax.experimental import pallas as pl
from jax.experimental.pallas import tpu as pltpu
from jax.sharding import Mesh, PartitionSpec as P

LAT = 512
ROPE = 64
VD = 128
NX, NZ, NY = 4, 4, 4
QUARTERS = NZ
CHIPS = NX * NZ * NY
GROUPS = NX * NZ
CHIP_AXES = ("x", "y", "z")
ALL_AXES = ("x", "z", "y", "core")
SWAP = [(0, 1), (1, 0)]
BF = jnp.bfloat16
F32 = jnp.float32


def swap(value):
    return lax.ppermute(value, "core", SWAP)


def exchange(value):
    return lax.all_to_all(value, CHIP_AXES, split_axis=0, concat_axis=0, tiled=True)


def limit(mib):
    return pltpu.CompilerParams(vmem_limit_bytes=mib * 1024 * 1024)


SENT_ROWS = 24
ROUTE_ROW = 8
STATE_ROW = 9


def attend_kernel(
    length_ref,
    query_hbm,
    cache_hbm,
    newest_hbm,
    states_hbm,
    ids_hbm,
    score_hbm,
    sent_ref,
    query_ref,
    cache_ref,
    newest_ref,
    states_ref,
    ids_ref,
    score_ref,
    latent_ref,
    pack_ref,
    done,
):
    copies = [
        pltpu.make_async_copy(source, target, done.at[index])
        for index, (source, target) in enumerate(
            (
                (cache_hbm, cache_ref),
                (query_hbm, query_ref),
                (newest_hbm, newest_ref),
                (states_hbm, states_ref),
                (ids_hbm, ids_ref),
                (score_hbm, score_ref),
            )
        )
    ]
    for copy in copies:
        copy.start()
    for copy in copies[3:]:
        copy.wait()
    lanes = 128
    pieces = states_ref[...].astype(F32)
    half = pieces.shape[1] // 2
    wide = half // QUARTERS
    tiles = wide // lanes
    for y in range(NY):
        for side in range(2):
            for t in range(tiles):
                at = side * half + y * wide + t * lanes
                row = y * SENT_ROWS + STATE_ROW + side * tiles + t
                pack_ref[row : row + 1, :] = pieces[:, at : at + lanes]
        pack_ref[(y + 1) * SENT_ROWS - 1 : (y + 1) * SENT_ROWS, :] = jnp.zeros((1, lanes), F32)
    first = pack_ref[: NY * SENT_ROWS, :]
    for g in range(1, GROUPS):
        pack_ref[g * NY * SENT_ROWS : (g + 1) * NY * SENT_ROWS, :] = first

    scores = score_ref[...]
    routes = (2.5 * scores / jnp.sum(scores, axis=1, keepdims=True)).astype(BF).astype(F32)
    ids = ids_ref[...]
    per_block = 3
    chip = lax.broadcasted_iota(jnp.int32, (CHIPS, lanes), 0)
    block = chip // (NY * NZ) * NZ + chip % NZ
    lane = lax.broadcasted_iota(jnp.int32, (CHIPS, lanes), 1)
    expert = jnp.where(lane < per_block, block * per_block + lane, -1)
    dense = jnp.zeros((CHIPS, lanes), F32)
    for k in range(ids.shape[1]):
        dense = dense + jnp.where(expert == ids[:, k : k + 1], routes[:, k : k + 1], 0.0)
    pack_ref[pl.ds(ROUTE_ROW, CHIPS, stride=SENT_ROWS), :] = dense

    for copy in copies[:3]:
        copy.wait()
    heads = query_ref.shape[1]
    positions = cache_ref.shape[1]
    softmax_scale = (VD + ROPE) ** (-0.5)
    contract_first = (((0,), (0,)), ((), ()))
    query = query_ref[...]
    cached = lax.dot_general(query, cache_ref[...], contract_first, preferred_element_type=F32)
    cached = cached * softmax_scale
    newest = newest_ref[...]
    newest_rows = jnp.broadcast_to(newest, (8, newest.shape[1]))
    own_score = lax.dot_general(
        query, newest_rows, (((0,), (1,)), ((), ())), preferred_element_type=F32
    )[:, :1]
    own_score = own_score * softmax_scale
    visible = lax.broadcasted_iota(jnp.int32, (heads, positions), 1) < length_ref[0]
    cached = jnp.where(visible, cached, -1e30)
    highest = jnp.maximum(jnp.max(cached, axis=1, keepdims=True), own_score)
    weights = jnp.where(visible, jnp.exp(cached - highest), 0.0)
    weight_own = jnp.exp(own_score - highest)
    denominator = jnp.sum(weights, axis=1, keepdims=True) + weight_own
    probs = (weights / denominator).astype(BF)
    prob_own = (weight_own / denominator).astype(BF).astype(F32)
    blended = lax.dot_general(
        probs, cache_ref[:LAT, :], (((1,), (1,)), ((), ())), preferred_element_type=F32
    )
    blended = blended + prob_own * newest[:, :LAT].astype(F32)
    for t in range(LAT // lanes):
        latent_ref[t] = blended[:, t * lanes : (t + 1) * lanes]

    for x in range(NX):
        for y in range(NY):
            head = 2 * (x * NZ * NY + y)
            row = (x * NY + y) * NZ * SENT_ROWS
            for t in range(LAT // lanes):
                for j in range(2):
                    piece = latent_ref[t, pl.ds(head + j, NZ, stride=2 * NY), :]
                    pack_ref[pl.ds(row + 2 * t + j, NZ, stride=SENT_ROWS), :] = piece
    sent_ref[...] = pack_ref[...].astype(BF).reshape(sent_ref.shape)


def attend_and_pack(lengths, queries, kv_cache, kv_new, states_in, expert_ids, route_scores):
    whole = pl.BlockSpec(memory_space=pltpu.VMEM)
    inputs = (queries[0].T, kv_cache[0].T, kv_new, states_in, expert_ids, route_scores)
    return pl.pallas_call(
        attend_kernel,
        in_specs=[pl.BlockSpec(memory_space=pltpu.SMEM)]
        + [pl.BlockSpec(memory_space=pltpu.HBM)] * len(inputs),
        out_specs=whole,
        out_shape=jax.ShapeDtypeStruct((CHIPS, SENT_ROWS, 128), BF),
        scratch_shapes=[pltpu.VMEM(value.shape, value.dtype) for value in inputs]
        + [
            pltpu.VMEM((LAT // 128, queries.shape[1], 128), F32),
            pltpu.VMEM((CHIPS * SENT_ROWS, 128), F32),
            pltpu.SemaphoreType.DMA((len(inputs),)),
        ],
        compiler_params=limit(62),
        name="attend",
    )(lengths, *inputs)


VALUE_ROWS = 3 * CHIPS + 32


def value_kernel(
    place_ref,
    got_ref,
    uv_own_hbm,
    uv_other_hbm,
    out_own_hbm,
    out_other_hbm,
    mine_ref,
    send_ref,
    weights_ref,
    own_ref,
    other_ref,
    rows_ref,
    state_ref,
    done,
):
    core = place_ref[0]
    heads = out_own_hbm.shape[0]
    half = weights_ref.shape[1]
    columns = pl.ds(pl.multiple_of(core * half, 128), half)
    copies = [
        pltpu.make_async_copy(source, target, done.at[index])
        for index, (source, target) in enumerate(
            (
                (uv_own_hbm, own_ref),
                (uv_other_hbm, other_ref),
                (out_own_hbm.at[:, columns], weights_ref.at[:heads]),
                (out_other_hbm.at[:, columns], weights_ref.at[heads:]),
            )
        )
    ]
    for copy in copies:
        copy.start()
    group = place_ref[1]
    lanes = 128
    rows_ref[...] = got_ref[...].astype(F32).reshape(rows_ref.shape)

    def latent(j):
        pieces = [
            rows_ref[pl.ds(2 * t + j, CHIPS, stride=SENT_ROWS), :].astype(BF) for t in range(LAT // lanes)
        ]
        return jnp.concatenate(pieces, axis=1)

    first, second = latent(0), latent(1)
    latent_own = jnp.where(core == 0, first, second)
    latent_other = jnp.where(core == 0, second, first)
    copies[0].wait()
    copies[1].wait()
    value_own = jnp.dot(latent_own, own_ref[...], preferred_element_type=F32).astype(BF)
    value_other = jnp.dot(latent_other, other_ref[...], preferred_element_type=F32).astype(BF)
    routes = rows_ref[pl.ds(ROUTE_ROW, CHIPS, stride=SENT_ROWS), :].astype(BF)
    base = pl.multiple_of(group * (NY * SENT_ROWS), 8)
    tiles = 7
    for side in range(2):
        state_ref[side] = jnp.zeros(state_ref.shape[1:], F32)
    for y in range(NY):
        source = rows_ref[pl.ds(base + y * SENT_ROWS, SENT_ROWS), :]
        for side in range(2):
            at = STATE_ROW + side * tiles
            state_ref[side, 8 * y : 8 * y + tiles, :] = source[at : at + tiles, :]
    low, high = state_ref[0], state_ref[1]
    for ref, a, b in ((mine_ref, value_own, value_other), (send_ref, value_other, value_own)):
        ref[:CHIPS, :] = a
        ref[CHIPS : 2 * CHIPS, :] = b
        ref[2 * CHIPS : 3 * CHIPS, :] = routes
    mine_ref[3 * CHIPS :, :] = jnp.where(core == 0, low, high).astype(BF)
    send_ref[3 * CHIPS :, :] = jnp.where(core == 0, high, low).astype(BF)
    copies[2].wait()
    copies[3].wait()


def project_values(place, got, uv_own, uv_other, out_own, out_other):
    whole = pl.BlockSpec(memory_space=pltpu.VMEM)
    outside = pl.BlockSpec(memory_space=pltpu.HBM)
    out = jax.ShapeDtypeStruct((VALUE_ROWS, 128), BF)
    heads, model = out_own.shape
    return pl.pallas_call(
        value_kernel,
        in_specs=[pl.BlockSpec(memory_space=pltpu.SMEM), whole] + [outside] * 4,
        out_specs=(whole, whole, whole),
        out_shape=(out, out, jax.ShapeDtypeStruct((2 * heads, model // 2), BF)),
        scratch_shapes=[
            pltpu.VMEM(uv_own.shape, BF),
            pltpu.VMEM(uv_own.shape, BF),
            pltpu.VMEM((CHIPS * SENT_ROWS, 128), F32),
            pltpu.VMEM((2, 32, 128), F32),
            pltpu.SemaphoreType.DMA((4,)),
        ],
        compiler_params=limit(12),
        name="values",
    )(place, got, uv_own, uv_other, out_own, out_other)


def out_kernel(
    place_ref, mine_ref, got_ref, weights_ref, out_ref, route_ref, states_ref, rows_ref, values_ref
):
    core = place_ref[0]
    lanes = 128
    mine = mine_ref[...].astype(F32)
    got = got_ref[...].astype(F32)
    even = jnp.where(core == 0, mine, got)
    odd = jnp.where(core == 0, got, mine)
    for part in range(3):
        rows = slice(part * CHIPS, (part + 1) * CHIPS)
        rows_ref[part, pl.ds(0, CHIPS, stride=2), :] = even[rows]
        rows_ref[part, pl.ds(1, CHIPS, stride=2), :] = odd[rows]
        if part < 2:
            values_ref[:, part * lanes : (part + 1) * lanes] = rows_ref[part].astype(BF)
        else:
            route_ref[...] = rows_ref[part]
    wide = states_ref.shape[1]
    for q in range(QUARTERS):
        for t in range(wide // lanes):
            at = 3 * CHIPS + 8 * q + t
            cols = slice(t * lanes, (t + 1) * lanes)
            states_ref[2 * q : 2 * q + 1, cols] = even[at : at + 1, :]
            states_ref[2 * q + 1 : 2 * q + 2, cols] = odd[at : at + 1, :]
    values = values_ref[...]
    groups = out_ref.shape[0]
    for q in range(QUARTERS):
        product = jnp.dot(values, weights_ref[:, q * wide : (q + 1) * wide], preferred_element_type=F32)
        out_ref[:, q] = product.astype(BF).reshape(groups, 8, wide)


def out_projection(place, mine, got, weights):
    rows = 2 * CHIPS
    wide = weights.shape[1] // QUARTERS
    whole = pl.BlockSpec(memory_space=pltpu.VMEM)
    return pl.pallas_call(
        out_kernel,
        in_specs=[pl.BlockSpec(memory_space=pltpu.SMEM), whole, whole, whole],
        out_specs=(whole, whole, whole),
        out_shape=(
            jax.ShapeDtypeStruct((rows // 8, QUARTERS, 8, wide), BF),
            jax.ShapeDtypeStruct((rows, 128), F32),
            jax.ShapeDtypeStruct((8, wide), F32),
        ),
        scratch_shapes=[pltpu.VMEM((3, rows, 128), F32), pltpu.VMEM((rows, 2 * VD), BF)],
        compiler_params=limit(12),
        name="out_projection",
    )(place, mine, got, weights)


def half_products(half, rows_ref, gain_ref, gate_ref, up_ref):
    groups, quarters, eight, wide = rows_ref.shape
    rows = groups * eight
    experts = gate_ref.shape[0]
    total = jnp.zeros((rows, 1), F32)
    sums = [None] * experts
    for pair in range(quarters // 2):
        pieces = [rows_ref[:, q].reshape(rows, wide) for q in (2 * pair, 2 * pair + 1)]
        piece = jnp.concatenate(pieces, axis=1).astype(F32)
        total = total + jnp.sum(piece * piece, axis=1, keepdims=True)
        at = pl.ds(pl.multiple_of(half * (quarters * wide) + pair * (2 * wide), 256), 2 * wide)
        scaled = (piece * gain_ref[:, at]).astype(BF)
        for e in range(experts):
            weights = jnp.concatenate([gate_ref[e, at, :], up_ref[e, at, :]], axis=1)
            product = jnp.dot(scaled, weights, preferred_element_type=F32)
            sums[e] = product if sums[e] is None else sums[e] + product
    return total, sums


def first_kernel(place_ref, rows_ref, gain_ref, gate_ref, up_ref, total_ref, sums_ref):
    total, sums = half_products(place_ref[0], rows_ref, gain_ref, gate_ref, up_ref)
    total_ref[...] = jnp.broadcast_to(total, total_ref.shape)
    for e, value in enumerate(sums):
        sums_ref[e] = value


def second_kernel(
    place_ref, rows_ref, gain_ref, gate_ref, up_ref, total_ref, sums_ref, route_ref, act_ref
):
    total, sums = half_products(1 - place_ref[0], rows_ref, gain_ref, gate_ref, up_ref)
    total = total + total_ref[:, :1]
    inverse = lax.rsqrt(total / gain_ref.shape[1] + 1e-06)
    hidden = gate_ref.shape[2]
    for e, value in enumerate(sums):
        value = (value + sums_ref[e]) * inverse
        gate = value[:, :hidden]
        active = gate / (1.0 + jnp.exp(-gate)) * value[:, hidden:]
        active = active * route_ref[:, e : e + 1]
        act_ref[:, e * hidden : (e + 1) * hidden] = active.astype(BF)


def gate_up(place, own, other, gain, route, w_gate, w_up):
    groups, _, eight, wide = own.shape
    rows = groups * eight
    experts, model, hidden = w_gate.shape
    whole = pl.BlockSpec(memory_space=pltpu.VMEM)
    where = pl.BlockSpec(memory_space=pltpu.SMEM)
    total, sums = pl.pallas_call(
        first_kernel,
        in_specs=[where] + [whole] * 4,
        out_specs=(whole, whole),
        out_shape=(
            jax.ShapeDtypeStruct((rows, 128), F32),
            jax.ShapeDtypeStruct((experts, rows, 2 * hidden), F32),
        ),
        compiler_params=limit(12),
        name="gate_up_first",
    )(place, own, gain[None], w_gate, w_up)
    return pl.pallas_call(
        second_kernel,
        in_specs=[where] + [whole] * 7,
        out_specs=whole,
        out_shape=jax.ShapeDtypeStruct((rows, experts * hidden), BF),
        compiler_params=limit(12),
        name="gate_up_second",
    )(place, other, gain[None], w_gate, w_up, total, sums, route)


DOWN_COLUMNS = 512


def down_kernel(place_ref, act_own_ref, act_other_ref, own_ref, other_ref, out_ref, sum_ref, pack_ref):
    core = place_ref[0]
    lanes = 128
    half = own_ref.shape[1] // 2
    act = jnp.concatenate([act_own_ref[...], act_other_ref[...]], axis=1)
    tiles = DOWN_COLUMNS // lanes
    for step in range(half // DOWN_COLUMNS):
        slot = step % 2
        at = pl.ds(pl.multiple_of(core * half + step * DOWN_COLUMNS, 512), DOWN_COLUMNS)
        weights = jnp.concatenate([own_ref[:, at], other_ref[:, at]], axis=0)
        product = jnp.dot(act, weights, preferred_element_type=F32)
        for t in range(tiles):
            sum_ref[slot, t] = product[:, t * lanes : (t + 1) * lanes]
            for j in range(2):
                piece = sum_ref[slot, t, pl.ds(j, CHIPS, stride=2), :]
                pack_ref[slot, pl.ds(2 * t + j, CHIPS, stride=2 * tiles), :] = piece
        rows = slice(step * 2 * tiles, (step + 1) * 2 * tiles)
        out_ref[:, rows, :] = pack_ref[slot].astype(BF).reshape(CHIPS, 2 * tiles, lanes)


def down(place, act_own, act_other, own, other):
    rows = act_own.shape[0]
    out_rows = own.shape[1] // 128
    tiles = DOWN_COLUMNS // 128
    whole = pl.BlockSpec(memory_space=pltpu.VMEM)
    return pl.pallas_call(
        down_kernel,
        in_specs=[pl.BlockSpec(memory_space=pltpu.SMEM)] + [whole] * 4,
        out_specs=whole,
        out_shape=jax.ShapeDtypeStruct((CHIPS, out_rows, 128), BF),
        scratch_shapes=[
            pltpu.VMEM((2, tiles, rows, 128), F32),
            pltpu.VMEM((2, CHIPS * 2 * tiles, 128), F32),
        ],
        compiler_params=limit(8),
        name="down",
    )(place, act_own, act_other, own, other)


def body(
    states_in,
    queries,
    kv_cache,
    kv_new,
    lengths,
    w_uv,
    w_out,
    norm_gain,
    expert_ids,
    route_scores,
    w_gate,
    w_up,
    w_down,
):
    core = lax.axis_index("core")
    group = lax.axis_index("x") * NY + lax.axis_index("y")
    quarter = lax.axis_index("z")
    model = states_in.shape[1]
    half = model // 2
    wide = half // QUARTERS
    down_own = w_down.reshape(-1, model)
    uv_other = swap(w_uv)
    out_other = swap(w_out)
    down_other = swap(down_own)
    place = jnp.stack([core, group])

    sent = attend_and_pack(
        lengths, queries, kv_cache, kv_new, states_in, expert_ids, route_scores
    )
    got = exchange(sent)
    mine, send, weights = project_values(place, got, w_uv[0], uv_other[0], w_out, out_other)
    partial, route, my_states = out_projection(place, mine, swap(send), weights)
    partial = exchange(partial.reshape(CHIPS, 8, wide))
    attention = jnp.sum(partial.astype(F32), axis=0)
    residual_part = (my_states + attention).astype(BF)
    rows_own = exchange(jnp.broadcast_to(residual_part[None], (CHIPS, 8, wide)))
    rows_other = swap(rows_own)
    rows_own = rows_own.reshape(GROUPS, NY, 8, wide)
    rows_other = rows_other.reshape(GROUPS, NY, 8, wide)

    act = gate_up(place, rows_own, rows_other, norm_gain, route, w_gate, w_up)
    act_other = swap(act)
    output = down(place, act, act_other, down_own, down_other)
    output = exchange(output)
    expert_sum = jnp.sum(output.astype(F32), axis=0)
    expert_sum = expert_sum.reshape(half // 128, 2, 128).transpose(1, 0, 2).reshape(2, half)

    def chip_rows(rows):
        mine = lax.dynamic_index_in_dim(rows, group, 0, keepdims=False)
        mine = lax.dynamic_slice_in_dim(mine, 2 * quarter, 2, 1)
        return mine.transpose(1, 0, 2).reshape(2, half)

    residual_own = chip_rows(rows_own)
    residual_other = chip_rows(rows_other)
    layer_half = (residual_own.astype(F32) + expert_sum).astype(BF)
    layer_mine = lax.dynamic_slice_in_dim(layer_half, core, 1, 0)
    layer_got = swap(lax.dynamic_slice_in_dim(layer_half, 1 - core, 1, 0))
    residual_mine = lax.dynamic_slice_in_dim(residual_own, core, 1, 0)
    residual_got = lax.dynamic_slice_in_dim(residual_other, core, 1, 0)

    def joined(mine, got):
        return jnp.where(
            core == 0, jnp.concatenate([mine, got], axis=1), jnp.concatenate([got, mine], axis=1)
        )

    return (joined(residual_mine, residual_got), joined(layer_mine, layer_got))


def solution(mesh):
    fine = Mesh(mesh.devices.reshape(NX, NZ, NY, 2), ALL_AXES)
    rows = P(ALL_AXES, None)
    cube = P(ALL_AXES, None, None)
    in_specs = (
        rows,
        cube,
        cube,
        rows,
        P(ALL_AXES),
        cube,
        rows,
        P(),
        rows,
        rows,
        P(("x", "z"), None, ("y", "core")),
        P(("x", "z"), None, ("y", "core")),
        P(("x", "z"), ("y", "core"), None),
    )
    return jax.shard_map(body, mesh=fine, in_specs=in_specs, out_specs=(rows, rows), check_vma=False)
```

```python
import jax
import jax.numpy as jnp
from jax import lax
from jax.experimental import pallas as pl
from jax.experimental.pallas import tpu as pltpu
from jax.sharding import Mesh, PartitionSpec as P

LAT = 512
ROPE = 64
VD = 128
NX, NZ, NY = 4, 4, 4
QUARTERS = NY
CHIPS = NX * NZ * NY
GROUPS = NX * NZ
CHIP_AXES = ("z", "x", "y")
ALL_AXES = ("x", "z", "y", "core")
SWAP = [(0, 1), (1, 0)]
BF = jnp.bfloat16
F32 = jnp.float32


def swap(value):
    return lax.ppermute(value, "core", SWAP)


def exchange(value):
    return lax.all_to_all(value, CHIP_AXES, split_axis=0, concat_axis=0, tiled=True)


def limit(mib):
    return pltpu.CompilerParams(vmem_limit_bytes=mib * 1024 * 1024)


SENT_ROWS = 24
ROUTE_ROW = 8
STATE_ROW = 9
CACHE_COPIES = 4


def attend_kernel(
    length_ref,
    query_hbm,
    cache_hbm,
    newest_hbm,
    states_hbm,
    ids_hbm,
    score_hbm,
    sent_ref,
    query_ref,
    cache_ref,
    newest_ref,
    states_ref,
    ids_ref,
    score_ref,
    latent_ref,
    pack_ref,
    done,
):
    piece = cache_hbm.shape[0] // CACHE_COPIES
    pairs = [
        (cache_hbm.at[k * piece : (k + 1) * piece], cache_ref.at[k * piece : (k + 1) * piece])
        for k in range(CACHE_COPIES)
    ]
    pairs += [(query_hbm, query_ref), (newest_hbm, newest_ref)]
    early = [(states_hbm, states_ref), (ids_hbm, ids_ref), (score_hbm, score_ref)]
    copies = [
        pltpu.make_async_copy(source, target, done.at[index])
        for index, (source, target) in enumerate(pairs + early)
    ]
    for copy in copies:
        copy.start()
    for copy in copies[len(pairs) :]:
        copy.wait()
    lanes = 128
    pieces = states_ref[...].astype(F32)
    half = pieces.shape[1] // 2
    wide = half // QUARTERS
    tiles = wide // lanes
    for y in range(NY):
        for side in range(2):
            for t in range(tiles):
                at = side * half + y * wide + t * lanes
                row = y * SENT_ROWS + STATE_ROW + side * tiles + t
                pack_ref[row : row + 1, :] = pieces[:, at : at + lanes]
        pack_ref[(y + 1) * SENT_ROWS - 1 : (y + 1) * SENT_ROWS, :] = jnp.zeros((1, lanes), F32)
    first = pack_ref[: NY * SENT_ROWS, :]
    for g in range(1, GROUPS):
        pack_ref[g * NY * SENT_ROWS : (g + 1) * NY * SENT_ROWS, :] = first

    scores = score_ref[...]
    routes = (2.5 * scores / jnp.sum(scores, axis=1, keepdims=True)).astype(BF).astype(F32)
    ids = ids_ref[...]
    per_block = 3
    chip = lax.broadcasted_iota(jnp.int32, (CHIPS, lanes), 0)
    block = chip // NY % NX * NZ + chip // (NX * NY)
    lane = lax.broadcasted_iota(jnp.int32, (CHIPS, lanes), 1)
    expert = jnp.where(lane < per_block, block * per_block + lane, -1)
    dense = jnp.zeros((CHIPS, lanes), F32)
    for k in range(ids.shape[1]):
        dense = dense + jnp.where(expert == ids[:, k : k + 1], routes[:, k : k + 1], 0.0)
    pack_ref[pl.ds(ROUTE_ROW, CHIPS, stride=SENT_ROWS), :] = dense

    for copy in copies[: len(pairs)]:
        copy.wait()
    heads = query_ref.shape[1]
    positions = cache_ref.shape[1]
    softmax_scale = (VD + ROPE) ** (-0.5)
    contract_first = (((0,), (0,)), ((), ()))
    query = query_ref[...]
    cached = lax.dot_general(query, cache_ref[...], contract_first, preferred_element_type=F32)
    cached = cached * softmax_scale
    newest = newest_ref[...]
    newest_rows = jnp.broadcast_to(newest, (8, newest.shape[1]))
    own_score = lax.dot_general(
        query, newest_rows, (((0,), (1,)), ((), ())), preferred_element_type=F32
    )[:, :1]
    own_score = own_score * softmax_scale
    visible = lax.broadcasted_iota(jnp.int32, (heads, positions), 1) < length_ref[0]
    cached = jnp.where(visible, cached, -1e30)
    highest = jnp.maximum(jnp.max(cached, axis=1, keepdims=True), own_score)
    weights = jnp.where(visible, jnp.exp(cached - highest), 0.0)
    weight_own = jnp.exp(own_score - highest)
    denominator = jnp.sum(weights, axis=1, keepdims=True) + weight_own
    probs = (weights / denominator).astype(BF)
    prob_own = (weight_own / denominator).astype(BF).astype(F32)
    blended = lax.dot_general(
        probs, cache_ref[:LAT, :], (((1,), (1,)), ((), ())), preferred_element_type=F32
    )
    blended = blended + prob_own * newest[:, :LAT].astype(F32)
    for t in range(LAT // lanes):
        latent_ref[t] = blended[:, t * lanes : (t + 1) * lanes]

    for x in range(NX):
        for z in range(NZ):
            head = 2 * (x * NZ + z) * NY
            row = (z * NX + x) * NY * SENT_ROWS
            for t in range(LAT // lanes):
                for j in range(2):
                    piece = latent_ref[t, pl.ds(head + j, NY, stride=2), :]
                    pack_ref[pl.ds(row + 2 * t + j, NY, stride=SENT_ROWS), :] = piece
    sent_ref[...] = pack_ref[...].astype(BF).reshape(sent_ref.shape)


def attend_and_pack(lengths, queries, kv_cache, kv_new, states_in, expert_ids, route_scores):
    whole = pl.BlockSpec(memory_space=pltpu.VMEM)
    inputs = (queries[0].T, kv_cache[0].T, kv_new, states_in, expert_ids, route_scores)
    return pl.pallas_call(
        attend_kernel,
        in_specs=[pl.BlockSpec(memory_space=pltpu.SMEM)]
        + [pl.BlockSpec(memory_space=pltpu.HBM)] * len(inputs),
        out_specs=whole,
        out_shape=jax.ShapeDtypeStruct((CHIPS, SENT_ROWS, 128), BF),
        scratch_shapes=[pltpu.VMEM(value.shape, value.dtype) for value in inputs]
        + [
            pltpu.VMEM((LAT // 128, queries.shape[1], 128), F32),
            pltpu.VMEM((CHIPS * SENT_ROWS, 128), F32),
            pltpu.SemaphoreType.DMA((len(inputs) + CACHE_COPIES - 1,)),
        ],
        compiler_params=limit(62),
        name="attend",
    )(lengths, *inputs)


VALUE_ROWS = 3 * CHIPS + 32


def value_kernel(place_ref, got_ref, uv_ref, after_ref, mine_ref, send_ref, rows_ref, state_ref):
    del after_ref
    core = place_ref[0]
    group = place_ref[1]
    lanes = 128
    rows_ref[...] = got_ref[...].astype(F32).reshape(rows_ref.shape)

    def latent(j):
        pieces = [
            rows_ref[pl.ds(2 * t + j, CHIPS, stride=SENT_ROWS), :].astype(BF) for t in range(LAT // lanes)
        ]
        return jnp.concatenate(pieces, axis=1)

    first, second = latent(0), latent(1)
    latent_own = jnp.where(core == 0, first, second)
    latent_other = jnp.where(core == 0, second, first)
    value_own = jnp.dot(latent_own, uv_ref[0], preferred_element_type=F32).astype(BF)
    value_other = jnp.dot(latent_other, uv_ref[1], preferred_element_type=F32).astype(BF)
    routes = rows_ref[pl.ds(ROUTE_ROW, CHIPS, stride=SENT_ROWS), :].astype(BF)
    base = pl.multiple_of(group * (NY * SENT_ROWS), 8)
    tiles = 7
    for side in range(2):
        state_ref[side] = jnp.zeros(state_ref.shape[1:], F32)
    for y in range(NY):
        source = rows_ref[pl.ds(base + y * SENT_ROWS, SENT_ROWS), :]
        for side in range(2):
            at = STATE_ROW + side * tiles
            state_ref[side, 8 * y : 8 * y + tiles, :] = source[at : at + tiles, :]
    low, high = state_ref[0], state_ref[1]
    for ref, a, b in ((mine_ref, value_own, value_other), (send_ref, value_other, value_own)):
        ref[:CHIPS, :] = a
        ref[CHIPS : 2 * CHIPS, :] = b
        ref[2 * CHIPS : 3 * CHIPS, :] = routes
    mine_ref[3 * CHIPS :, :] = jnp.where(core == 0, low, high).astype(BF)
    send_ref[3 * CHIPS :, :] = jnp.where(core == 0, high, low).astype(BF)


def project_values(place, got, uv, after):
    whole = pl.BlockSpec(memory_space=pltpu.VMEM)
    out = jax.ShapeDtypeStruct((VALUE_ROWS, 128), BF)
    return pl.pallas_call(
        value_kernel,
        in_specs=[
            pl.BlockSpec(memory_space=pltpu.SMEM),
            whole,
            whole,
            pl.BlockSpec(memory_space=pl.ANY),
        ],
        out_specs=(whole, whole),
        out_shape=(out, out),
        scratch_shapes=[
            pltpu.VMEM((CHIPS * SENT_ROWS, 128), F32),
            pltpu.VMEM((2, 32, 128), F32),
        ],
        compiler_params=limit(12),
        name="values",
    )(place, got, uv, after)


def fetch_kernel(
    place_ref,
    uv_own_hbm,
    uv_other_hbm,
    own_hbm,
    other_hbm,
    uv_ref,
    weights_ref,
    done,
):
    heads = own_hbm.shape[0]
    half = weights_ref.shape[1]
    columns = pl.ds(pl.multiple_of(place_ref[0] * half, 128), half)
    copies = [
        pltpu.make_async_copy(source, target, done.at[index])
        for index, (source, target) in enumerate(
            (
                (uv_own_hbm, uv_ref.at[0]),
                (uv_other_hbm, uv_ref.at[1]),
                (own_hbm.at[:, columns], weights_ref.at[:heads]),
                (other_hbm.at[:, columns], weights_ref.at[heads:]),
            )
        )
    ]
    for copy in copies:
        copy.start()
    for copy in copies:
        copy.wait()


def fetch_halves(place, uv_own, uv_other, own, other):
    whole = pl.BlockSpec(memory_space=pltpu.VMEM)
    return pl.pallas_call(
        fetch_kernel,
        in_specs=[pl.BlockSpec(memory_space=pltpu.SMEM)]
        + [pl.BlockSpec(memory_space=pl.ANY)] * 4,
        out_specs=(whole, whole),
        out_shape=(
            jax.ShapeDtypeStruct((2,) + uv_own.shape, BF),
            jax.ShapeDtypeStruct((2 * own.shape[0], own.shape[1] // 2), BF),
        ),
        scratch_shapes=[pltpu.SemaphoreType.DMA((4,))],
        compiler_params=limit(4),
        name="fetch",
    )(place, uv_own, uv_other, own, other)


def out_kernel(
    place_ref, mine_ref, got_ref, weights_ref, out_ref, route_ref, states_ref, rows_ref, values_ref
):
    core = place_ref[0]
    lanes = 128
    mine = mine_ref[...].astype(F32)
    got = got_ref[...].astype(F32)
    even = jnp.where(core == 0, mine, got)
    odd = jnp.where(core == 0, got, mine)
    for part in range(3):
        rows = slice(part * CHIPS, (part + 1) * CHIPS)
        rows_ref[part, pl.ds(0, CHIPS, stride=2), :] = even[rows]
        rows_ref[part, pl.ds(1, CHIPS, stride=2), :] = odd[rows]
        if part < 2:
            values_ref[:, part * lanes : (part + 1) * lanes] = rows_ref[part].astype(BF)
        else:
            route_ref[...] = rows_ref[part]
    wide = states_ref.shape[1]
    for q in range(QUARTERS):
        for t in range(wide // lanes):
            at = 3 * CHIPS + 8 * q + t
            cols = slice(t * lanes, (t + 1) * lanes)
            states_ref[2 * q : 2 * q + 1, cols] = even[at : at + 1, :]
            states_ref[2 * q + 1 : 2 * q + 2, cols] = odd[at : at + 1, :]
    values = values_ref[...]
    groups = out_ref.shape[0]
    for q in range(QUARTERS):
        product = jnp.dot(values, weights_ref[:, q * wide : (q + 1) * wide], preferred_element_type=F32)
        out_ref[:, q] = product.astype(BF).reshape(groups, 8, wide)


def out_projection(place, mine, got, weights):
    rows = 2 * CHIPS
    wide = weights.shape[1] // QUARTERS
    whole = pl.BlockSpec(memory_space=pltpu.VMEM)
    return pl.pallas_call(
        out_kernel,
        in_specs=[pl.BlockSpec(memory_space=pltpu.SMEM), whole, whole, whole],
        out_specs=(whole, whole, whole),
        out_shape=(
            jax.ShapeDtypeStruct((rows // 8, QUARTERS, 8, wide), BF),
            jax.ShapeDtypeStruct((rows, 128), F32),
            jax.ShapeDtypeStruct((8, wide), F32),
        ),
        scratch_shapes=[pltpu.VMEM((3, rows, 128), F32), pltpu.VMEM((rows, 2 * VD), BF)],
        compiler_params=limit(12),
        name="out_projection",
    )(place, mine, got, weights)


def half_products(half, rows_ref, gain_ref, gate_ref, up_ref):
    groups, quarters, eight, wide = rows_ref.shape
    rows = groups * eight
    experts = gate_ref.shape[0]
    total = jnp.zeros((rows, 1), F32)
    sums = [None] * experts
    for pair in range(quarters // 2):
        pieces = [rows_ref[:, q].reshape(rows, wide) for q in (2 * pair, 2 * pair + 1)]
        piece = jnp.concatenate(pieces, axis=1).astype(F32)
        total = total + jnp.sum(piece * piece, axis=1, keepdims=True)
        at = pl.ds(pl.multiple_of(half * (quarters * wide) + pair * (2 * wide), 256), 2 * wide)
        scaled = (piece * gain_ref[:, at]).astype(BF)
        for e in range(experts):
            weights = jnp.concatenate([gate_ref[e, at, :], up_ref[e, at, :]], axis=1)
            product = jnp.dot(scaled, weights, preferred_element_type=F32)
            sums[e] = product if sums[e] is None else sums[e] + product
    return total, sums


COPIES = 6


def first_kernel(
    place_ref, rows_ref, gain_ref, gate_ref, up_ref, down_hbm, total_ref, sums_ref, down_ref, done
):
    half = down_ref.shape[1]
    columns = pl.ds(pl.multiple_of(place_ref[0] * half, 128), half)
    piece = down_ref.shape[0] // COPIES
    copies = [
        pltpu.make_async_copy(
            down_hbm.at[index * piece : (index + 1) * piece, columns],
            down_ref.at[index * piece : (index + 1) * piece],
            done.at[index],
        )
        for index in range(COPIES)
    ]
    for copy in copies:
        copy.start()
    total, sums = half_products(place_ref[0], rows_ref, gain_ref, gate_ref, up_ref)
    total_ref[...] = jnp.broadcast_to(total, total_ref.shape)
    for e, value in enumerate(sums):
        sums_ref[e] = value
    for copy in copies:
        copy.wait()


def second_kernel(
    place_ref, rows_ref, gain_ref, gate_ref, up_ref, total_ref, sums_ref, route_ref, act_ref
):
    total, sums = half_products(1 - place_ref[0], rows_ref, gain_ref, gate_ref, up_ref)
    total = total + total_ref[:, :1]
    inverse = lax.rsqrt(total / gain_ref.shape[1] + 1e-06)
    hidden = gate_ref.shape[2]
    for e, value in enumerate(sums):
        value = (value + sums_ref[e]) * inverse
        gate = value[:, :hidden]
        active = gate / (1.0 + jnp.exp(-gate)) * value[:, hidden:]
        active = active * route_ref[:, e : e + 1]
        act_ref[:, e * hidden : (e + 1) * hidden] = active.astype(BF)


def gate_up(place, own, other, gain, route, w_gate, w_up, down_other):
    groups, _, eight, wide = own.shape
    rows = groups * eight
    experts, model, hidden = w_gate.shape
    whole = pl.BlockSpec(memory_space=pltpu.VMEM)
    where = pl.BlockSpec(memory_space=pltpu.SMEM)
    down_rows, down_columns = down_other.shape
    total, sums, down_half = pl.pallas_call(
        first_kernel,
        in_specs=[where] + [whole] * 4 + [pl.BlockSpec(memory_space=pltpu.HBM)],
        out_specs=(whole, whole, whole),
        out_shape=(
            jax.ShapeDtypeStruct((rows, 128), F32),
            jax.ShapeDtypeStruct((experts, rows, 2 * hidden), F32),
            jax.ShapeDtypeStruct((down_rows, down_columns // 2), BF),
        ),
        scratch_shapes=[pltpu.SemaphoreType.DMA((COPIES,))],
        compiler_params=limit(12),
        name="gate_up_first",
    )(place, own, gain[None], w_gate, w_up, down_other)
    act = pl.pallas_call(
        second_kernel,
        in_specs=[where] + [whole] * 7,
        out_specs=whole,
        out_shape=jax.ShapeDtypeStruct((rows, experts * hidden), BF),
        compiler_params=limit(12),
        name="gate_up_second",
    )(place, other, gain[None], w_gate, w_up, total, sums, route)
    return act, down_half


DOWN_COLUMNS = 512


def down_kernel(place_ref, act_own_ref, act_other_ref, own_ref, other_ref, out_ref, sum_ref, pack_ref):
    core = place_ref[0]
    lanes = 128
    half = own_ref.shape[1] // 2
    act = jnp.concatenate([act_own_ref[...], act_other_ref[...]], axis=1)
    tiles = DOWN_COLUMNS // lanes
    for step in range(half // DOWN_COLUMNS):
        slot = step % 2
        at = pl.ds(pl.multiple_of(core * half + step * DOWN_COLUMNS, 512), DOWN_COLUMNS)
        other = other_ref[:, step * DOWN_COLUMNS : (step + 1) * DOWN_COLUMNS]
        weights = jnp.concatenate([own_ref[:, at], other], axis=0)
        product = jnp.dot(act, weights, preferred_element_type=F32)
        for t in range(tiles):
            sum_ref[slot, t] = product[:, t * lanes : (t + 1) * lanes]
            for j in range(2):
                piece = sum_ref[slot, t, pl.ds(j, CHIPS, stride=2), :]
                pack_ref[slot, pl.ds(2 * t + j, CHIPS, stride=2 * tiles), :] = piece
        rows = slice(step * 2 * tiles, (step + 1) * 2 * tiles)
        out_ref[:, rows, :] = pack_ref[slot].astype(BF).reshape(CHIPS, 2 * tiles, lanes)


def down(place, act_own, act_other, own, other):
    rows = act_own.shape[0]
    out_rows = own.shape[1] // 128
    tiles = DOWN_COLUMNS // 128
    whole = pl.BlockSpec(memory_space=pltpu.VMEM)
    return pl.pallas_call(
        down_kernel,
        in_specs=[pl.BlockSpec(memory_space=pltpu.SMEM)] + [whole] * 4,
        out_specs=whole,
        out_shape=jax.ShapeDtypeStruct((CHIPS, out_rows, 128), BF),
        scratch_shapes=[
            pltpu.VMEM((2, tiles, rows, 128), F32),
            pltpu.VMEM((2, CHIPS * 2 * tiles, 128), F32),
        ],
        compiler_params=limit(8),
        name="down",
    )(place, act_own, act_other, own, other)


def rows_kernel(place_ref, own_ref, other_ref, after_ref, residual_ref, rows_ref):
    del after_ref
    core = place_ref[0]
    group = place_ref[1]
    quarter = place_ref[2]
    quarters, wide = own_ref.shape[1], own_ref.shape[3]
    half = quarters * wide
    place = lax.broadcasted_iota(jnp.int32, (8, wide), 0)
    for q in range(quarters):
        cols = slice(q * wide, (q + 1) * wide)

        def row(ref, at):
            block = ref[group, q].astype(F32)
            return jnp.sum(jnp.where(place == at, block, 0.0), axis=0, keepdims=True)

        first, second = row(own_ref, 2 * quarter), row(own_ref, 2 * quarter + 1)
        rows_ref[0:1, cols] = first
        rows_ref[1:2, cols] = second
        at = pl.ds(pl.multiple_of(core * half + q * wide, 128), wide)
        residual_ref[:, at] = jnp.where(core == 0, first, second).astype(BF)
        at = pl.ds(pl.multiple_of((1 - core) * half + q * wide, 128), wide)
        residual_ref[:, at] = row(other_ref, 2 * quarter + core).astype(BF)


def take_rows(place, own, other, after):
    half = own.shape[1] * own.shape[3]
    whole = pl.BlockSpec(memory_space=pltpu.VMEM)
    return pl.pallas_call(
        rows_kernel,
        in_specs=[
            pl.BlockSpec(memory_space=pltpu.SMEM),
            whole,
            whole,
            pl.BlockSpec(memory_space=pl.ANY),
        ],
        out_specs=(whole, whole),
        out_shape=(
            jax.ShapeDtypeStruct((1, 2 * half), BF),
            jax.ShapeDtypeStruct((2, half), F32),
        ),
        compiler_params=limit(4),
        name="take_rows",
    )(place, own, other, after)


def finish_kernel(place_ref, got_ref, rows_ref, mine_ref, send_ref, sum_ref):
    core = place_ref[0]
    lanes = 128
    sum_ref[...] = jnp.sum(got_ref[...].astype(F32), axis=0)
    for tile in range(rows_ref.shape[1] // lanes):
        cols = slice(tile * lanes, (tile + 1) * lanes)
        both = rows_ref[:, cols] + sum_ref[2 * tile : 2 * tile + 2, :]
        mine_ref[:, cols] = jnp.where(core == 0, both[:1], both[1:]).astype(BF)
        send_ref[:, cols] = jnp.where(core == 0, both[1:], both[:1]).astype(BF)


def finish(place, got, rows):
    whole = pl.BlockSpec(memory_space=pltpu.VMEM)
    part = jax.ShapeDtypeStruct((1, rows.shape[1]), BF)
    return pl.pallas_call(
        finish_kernel,
        in_specs=[pl.BlockSpec(memory_space=pltpu.SMEM)] + [whole] * 2,
        out_specs=(whole, whole),
        out_shape=(part, part),
        scratch_shapes=[pltpu.VMEM(got.shape[1:], F32)],
        compiler_params=limit(4),
        name="finish",
    )(place, got, rows)


def body(
    states_in,
    queries,
    kv_cache,
    kv_new,
    lengths,
    w_uv,
    w_out,
    norm_gain,
    expert_ids,
    route_scores,
    w_gate,
    w_up,
    w_down,
):
    core = lax.axis_index("core")
    group = lax.axis_index("z") * NX + lax.axis_index("x")
    quarter = lax.axis_index("y")
    model = states_in.shape[1]
    half = model // 2
    wide = half // QUARTERS
    down_own = w_down.reshape(-1, model)
    uv_other = swap(w_uv)
    out_other = swap(w_out)
    down_other = swap(down_own)
    place = jnp.stack([core, group, quarter])

    sent = attend_and_pack(
        lengths, queries, kv_cache, kv_new, states_in, expert_ids, route_scores
    )
    got = exchange(sent)
    uv, weights = fetch_halves(place, w_uv[0], uv_other[0], w_out, out_other)
    mine, send = project_values(place, got, uv, weights)
    partial, route, my_states = out_projection(place, mine, swap(send), weights)
    partial = exchange(partial.reshape(CHIPS, 8, wide))
    attention = jnp.sum(partial.astype(F32), axis=0)
    residual_part = (my_states + attention).astype(BF)
    rows_own = exchange(jnp.broadcast_to(residual_part[None], (CHIPS, 8, wide)))
    rows_other = swap(rows_own)
    rows_own = rows_own.reshape(GROUPS, NY, 8, wide)
    rows_other = rows_other.reshape(GROUPS, NY, 8, wide)

    act, down_half = gate_up(
        place, rows_own, rows_other, norm_gain, route, w_gate, w_up, down_other
    )
    residual, chip_rows = take_rows(place, rows_own, rows_other, act)
    output = down(place, act, swap(act), down_own, down_half)
    mine, send = finish(place, exchange(output), chip_rows)
    got = swap(send)
    layer_out = jnp.where(
        core == 0, jnp.concatenate([mine, got], axis=1), jnp.concatenate([got, mine], axis=1)
    )
    return (residual, layer_out)


def solution(mesh):
    fine = Mesh(mesh.devices.reshape(NX, NZ, NY, 2), ALL_AXES)
    rows = P(ALL_AXES, None)
    cube = P(ALL_AXES, None, None)
    in_specs = (
        rows,
        cube,
        cube,
        rows,
        P(ALL_AXES),
        cube,
        rows,
        P(),
        rows,
        rows,
        P(("x", "z"), None, ("y", "core")),
        P(("x", "z"), None, ("y", "core")),
        P(("x", "z"), ("y", "core"), None),
    )
    return jax.shard_map(body, mesh=fine, in_specs=in_specs, out_specs=(rows, rows), check_vma=False)
```

```python
import jax
import jax.numpy as jnp
from jax import lax
from jax.experimental import pallas as pl
from jax.experimental.pallas import tpu as pltpu
from jax.sharding import Mesh, PartitionSpec as P

LAT = 512
ROPE = 64
VD = 128
NX, NZ, NY = 4, 4, 4
QUARTERS = NY
CHIPS = NX * NZ * NY
GROUPS = NX * NZ
CHIP_AXES = ("z", "x", "y")
ALL_AXES = ("x", "z", "y", "core")
SWAP = [(0, 1), (1, 0)]
BF = jnp.bfloat16
F32 = jnp.float32


def swap(value):
    return lax.ppermute(value, "core", SWAP)


def exchange(value):
    return lax.all_to_all(value, CHIP_AXES, split_axis=0, concat_axis=0, tiled=True)


def limit(mib):
    return pltpu.CompilerParams(vmem_limit_bytes=mib * 1024 * 1024)


SENT_ROWS = 24
ROUTE_ROW = 8
STATE_ROW = 9
CACHE_COPIES = 4


def attend_kernel(
    length_ref,
    query_hbm,
    cache_hbm,
    newest_hbm,
    states_hbm,
    ids_hbm,
    score_hbm,
    sent_ref,
    query_ref,
    cache_ref,
    newest_ref,
    states_ref,
    ids_ref,
    score_ref,
    latent_ref,
    pack_ref,
    done,
):
    piece = cache_hbm.shape[0] // CACHE_COPIES
    pairs = [
        (cache_hbm.at[k * piece : (k + 1) * piece], cache_ref.at[k * piece : (k + 1) * piece])
        for k in range(CACHE_COPIES)
    ]
    pairs += [(query_hbm, query_ref), (newest_hbm, newest_ref)]
    early = [(states_hbm, states_ref), (ids_hbm, ids_ref), (score_hbm, score_ref)]
    copies = [
        pltpu.make_async_copy(source, target, done.at[index])
        for index, (source, target) in enumerate(pairs + early)
    ]
    for copy in copies:
        copy.start()
    for copy in copies[len(pairs) :]:
        copy.wait()
    lanes = 128
    pieces = states_ref[...].astype(F32)
    half = pieces.shape[1] // 2
    wide = half // QUARTERS
    tiles = wide // lanes
    for y in range(NY):
        for side in range(2):
            for t in range(tiles):
                at = side * half + y * wide + t * lanes
                row = y * SENT_ROWS + STATE_ROW + side * tiles + t
                pack_ref[row : row + 1, :] = pieces[:, at : at + lanes]
        pack_ref[(y + 1) * SENT_ROWS - 1 : (y + 1) * SENT_ROWS, :] = jnp.zeros((1, lanes), F32)
    first = pack_ref[: NY * SENT_ROWS, :]
    for g in range(1, GROUPS):
        pack_ref[g * NY * SENT_ROWS : (g + 1) * NY * SENT_ROWS, :] = first

    scores = score_ref[...]
    routes = (2.5 * scores / jnp.sum(scores, axis=1, keepdims=True)).astype(BF).astype(F32)
    ids = ids_ref[...]
    per_block = 3
    chip = lax.broadcasted_iota(jnp.int32, (CHIPS, lanes), 0)
    block = chip // NY % NX * NZ + chip // (NX * NY)
    lane = lax.broadcasted_iota(jnp.int32, (CHIPS, lanes), 1)
    expert = jnp.where(lane < per_block, block * per_block + lane, -1)
    dense = jnp.zeros((CHIPS, lanes), F32)
    for k in range(ids.shape[1]):
        dense = dense + jnp.where(expert == ids[:, k : k + 1], routes[:, k : k + 1], 0.0)
    pack_ref[pl.ds(ROUTE_ROW, CHIPS, stride=SENT_ROWS), :] = dense

    for copy in copies[: len(pairs)]:
        copy.wait()
    heads = query_ref.shape[1]
    positions = cache_ref.shape[1]
    softmax_scale = (VD + ROPE) ** (-0.5)
    contract_first = (((0,), (0,)), ((), ()))
    query = query_ref[...]
    cached = lax.dot_general(query, cache_ref[...], contract_first, preferred_element_type=F32)
    cached = cached * softmax_scale
    newest = newest_ref[...]
    newest_rows = jnp.broadcast_to(newest, (8, newest.shape[1]))
    own_score = lax.dot_general(
        query, newest_rows, (((0,), (1,)), ((), ())), preferred_element_type=F32
    )[:, :1]
    own_score = own_score * softmax_scale
    visible = lax.broadcasted_iota(jnp.int32, (heads, positions), 1) < length_ref[0]
    cached = jnp.where(visible, cached, -1e30)
    highest = jnp.maximum(jnp.max(cached, axis=1, keepdims=True), own_score)
    weights = jnp.where(visible, jnp.exp(cached - highest), 0.0)
    weight_own = jnp.exp(own_score - highest)
    denominator = jnp.sum(weights, axis=1, keepdims=True) + weight_own
    probs = (weights / denominator).astype(BF)
    prob_own = (weight_own / denominator).astype(BF).astype(F32)
    blended = lax.dot_general(
        probs, cache_ref[:LAT, :], (((1,), (1,)), ((), ())), preferred_element_type=F32
    )
    blended = blended + prob_own * newest[:, :LAT].astype(F32)
    for t in range(LAT // lanes):
        latent_ref[t] = blended[:, t * lanes : (t + 1) * lanes]

    for x in range(NX):
        for z in range(NZ):
            head = 2 * (x * NZ + z) * NY
            row = (z * NX + x) * NY * SENT_ROWS
            for t in range(LAT // lanes):
                for j in range(2):
                    piece = latent_ref[t, pl.ds(head + j, NY, stride=2), :]
                    pack_ref[pl.ds(row + 2 * t + j, NY, stride=SENT_ROWS), :] = piece
    sent_ref[...] = pack_ref[...].astype(BF).reshape(sent_ref.shape)


def attend_and_pack(lengths, queries, kv_cache, kv_new, states_in, expert_ids, route_scores):
    whole = pl.BlockSpec(memory_space=pltpu.VMEM)
    inputs = (queries[0].T, kv_cache[0].T, kv_new, states_in, expert_ids, route_scores)
    return pl.pallas_call(
        attend_kernel,
        in_specs=[pl.BlockSpec(memory_space=pltpu.SMEM)]
        + [pl.BlockSpec(memory_space=pltpu.HBM)] * len(inputs),
        out_specs=whole,
        out_shape=jax.ShapeDtypeStruct((CHIPS, SENT_ROWS, 128), BF),
        scratch_shapes=[pltpu.VMEM(value.shape, value.dtype) for value in inputs]
        + [
            pltpu.VMEM((LAT // 128, queries.shape[1], 128), F32),
            pltpu.VMEM((CHIPS * SENT_ROWS, 128), F32),
            pltpu.SemaphoreType.DMA((len(inputs) + CACHE_COPIES - 1,)),
        ],
        compiler_params=limit(62),
        name="attend",
    )(lengths, *inputs)


VALUE_ROWS = 3 * CHIPS + 32


def value_kernel(place_ref, got_ref, uv_ref, after_ref, mine_ref, send_ref, rows_ref, state_ref):
    del after_ref
    core = place_ref[0]
    group = place_ref[1]
    lanes = 128
    rows_ref[...] = got_ref[...].astype(F32).reshape(rows_ref.shape)

    def latent(j):
        pieces = [
            rows_ref[pl.ds(2 * t + j, CHIPS, stride=SENT_ROWS), :].astype(BF) for t in range(LAT // lanes)
        ]
        return jnp.concatenate(pieces, axis=1)

    first, second = latent(0), latent(1)
    latent_own = jnp.where(core == 0, first, second)
    latent_other = jnp.where(core == 0, second, first)
    value_own = jnp.dot(latent_own, uv_ref[0], preferred_element_type=F32).astype(BF)
    value_other = jnp.dot(latent_other, uv_ref[1], preferred_element_type=F32).astype(BF)
    routes = rows_ref[pl.ds(ROUTE_ROW, CHIPS, stride=SENT_ROWS), :].astype(BF)
    base = pl.multiple_of(group * (NY * SENT_ROWS), 8)
    tiles = 7
    for side in range(2):
        state_ref[side] = jnp.zeros(state_ref.shape[1:], F32)
    for y in range(NY):
        source = rows_ref[pl.ds(base + y * SENT_ROWS, SENT_ROWS), :]
        for side in range(2):
            at = STATE_ROW + side * tiles
            state_ref[side, 8 * y : 8 * y + tiles, :] = source[at : at + tiles, :]
    low, high = state_ref[0], state_ref[1]
    for ref, a, b in ((mine_ref, value_own, value_other), (send_ref, value_other, value_own)):
        ref[:CHIPS, :] = a
        ref[CHIPS : 2 * CHIPS, :] = b
        ref[2 * CHIPS : 3 * CHIPS, :] = routes
    mine_ref[3 * CHIPS :, :] = jnp.where(core == 0, low, high).astype(BF)
    send_ref[3 * CHIPS :, :] = jnp.where(core == 0, high, low).astype(BF)


def project_values(place, got, uv, after):
    whole = pl.BlockSpec(memory_space=pltpu.VMEM)
    out = jax.ShapeDtypeStruct((VALUE_ROWS, 128), BF)
    return pl.pallas_call(
        value_kernel,
        in_specs=[
            pl.BlockSpec(memory_space=pltpu.SMEM),
            whole,
            whole,
            pl.BlockSpec(memory_space=pl.ANY),
        ],
        out_specs=(whole, whole),
        out_shape=(out, out),
        scratch_shapes=[
            pltpu.VMEM((CHIPS * SENT_ROWS, 128), F32),
            pltpu.VMEM((2, 32, 128), F32),
        ],
        compiler_params=limit(12),
        name="values",
    )(place, got, uv, after)


def fetch_kernel(
    place_ref,
    uv_own_hbm,
    uv_other_hbm,
    own_hbm,
    other_hbm,
    uv_ref,
    weights_ref,
    done,
):
    heads = own_hbm.shape[0]
    half = weights_ref.shape[1]
    columns = pl.ds(pl.multiple_of(place_ref[0] * half, 128), half)
    copies = [
        pltpu.make_async_copy(source, target, done.at[index])
        for index, (source, target) in enumerate(
            (
                (uv_own_hbm, uv_ref.at[0]),
                (uv_other_hbm, uv_ref.at[1]),
                (own_hbm.at[:, columns], weights_ref.at[:heads]),
                (other_hbm.at[:, columns], weights_ref.at[heads:]),
            )
        )
    ]
    for copy in copies:
        copy.start()
    for copy in copies:
        copy.wait()


def fetch_halves(place, uv_own, uv_other, own, other):
    whole = pl.BlockSpec(memory_space=pltpu.VMEM)
    return pl.pallas_call(
        fetch_kernel,
        in_specs=[pl.BlockSpec(memory_space=pltpu.SMEM)]
        + [pl.BlockSpec(memory_space=pl.ANY)] * 4,
        out_specs=(whole, whole),
        out_shape=(
            jax.ShapeDtypeStruct((2,) + uv_own.shape, BF),
            jax.ShapeDtypeStruct((2 * own.shape[0], own.shape[1] // 2), BF),
        ),
        scratch_shapes=[pltpu.SemaphoreType.DMA((4,))],
        compiler_params=limit(4),
        name="fetch",
    )(place, uv_own, uv_other, own, other)


def out_kernel(
    place_ref, mine_ref, got_ref, weights_ref, out_ref, route_ref, states_ref, rows_ref, values_ref
):
    core = place_ref[0]
    lanes = 128
    mine = mine_ref[...].astype(F32)
    got = got_ref[...].astype(F32)
    even = jnp.where(core == 0, mine, got)
    odd = jnp.where(core == 0, got, mine)
    for part in range(3):
        rows = slice(part * CHIPS, (part + 1) * CHIPS)
        rows_ref[part, pl.ds(0, CHIPS, stride=2), :] = even[rows]
        rows_ref[part, pl.ds(1, CHIPS, stride=2), :] = odd[rows]
        if part < 2:
            values_ref[:, part * lanes : (part + 1) * lanes] = rows_ref[part].astype(BF)
        else:
            route_ref[...] = rows_ref[part]
    wide = states_ref.shape[1]
    for q in range(QUARTERS):
        for t in range(wide // lanes):
            at = 3 * CHIPS + 8 * q + t
            cols = slice(t * lanes, (t + 1) * lanes)
            states_ref[2 * q : 2 * q + 1, cols] = even[at : at + 1, :]
            states_ref[2 * q + 1 : 2 * q + 2, cols] = odd[at : at + 1, :]
    values = values_ref[...]
    groups = out_ref.shape[0]
    for q in range(QUARTERS):
        product = jnp.dot(values, weights_ref[:, q * wide : (q + 1) * wide], preferred_element_type=F32)
        out_ref[:, q] = product.astype(BF).reshape(groups, 8, wide)


def out_projection(place, mine, got, weights):
    rows = 2 * CHIPS
    wide = weights.shape[1] // QUARTERS
    whole = pl.BlockSpec(memory_space=pltpu.VMEM)
    return pl.pallas_call(
        out_kernel,
        in_specs=[pl.BlockSpec(memory_space=pltpu.SMEM), whole, whole, whole],
        out_specs=(whole, whole, whole),
        out_shape=(
            jax.ShapeDtypeStruct((rows // 8, QUARTERS, 8, wide), BF),
            jax.ShapeDtypeStruct((rows, 128), F32),
            jax.ShapeDtypeStruct((8, wide), F32),
        ),
        scratch_shapes=[pltpu.VMEM((3, rows, 128), F32), pltpu.VMEM((rows, 2 * VD), BF)],
        compiler_params=limit(12),
        name="out_projection",
    )(place, mine, got, weights)


def half_products(half, rows_ref, gain_ref, gate_ref, up_ref):
    groups, quarters, eight, wide = rows_ref.shape
    rows = groups * eight
    experts = gate_ref.shape[0]
    total = jnp.zeros((rows, 1), F32)
    sums = [None] * experts
    for pair in range(quarters // 2):
        pieces = [rows_ref[:, q].reshape(rows, wide) for q in (2 * pair, 2 * pair + 1)]
        piece = jnp.concatenate(pieces, axis=1).astype(F32)
        total = total + jnp.sum(piece * piece, axis=1, keepdims=True)
        at = pl.ds(pl.multiple_of(half * (quarters * wide) + pair * (2 * wide), 256), 2 * wide)
        scaled = (piece * gain_ref[:, at]).astype(BF)
        for e in range(experts):
            weights = jnp.concatenate([gate_ref[e, at, :], up_ref[e, at, :]], axis=1)
            product = jnp.dot(scaled, weights, preferred_element_type=F32)
            sums[e] = product if sums[e] is None else sums[e] + product
    return total, sums


COPIES = 6


def first_kernel(
    place_ref, rows_ref, gain_ref, gate_ref, up_ref, down_hbm, total_ref, sums_ref, down_ref, done
):
    half = down_ref.shape[1]
    columns = pl.ds(pl.multiple_of(place_ref[0] * half, 128), half)
    piece = down_ref.shape[0] // COPIES
    copies = [
        pltpu.make_async_copy(
            down_hbm.at[index * piece : (index + 1) * piece, columns],
            down_ref.at[index * piece : (index + 1) * piece],
            done.at[index],
        )
        for index in range(COPIES)
    ]
    for copy in copies:
        copy.start()
    total, sums = half_products(place_ref[0], rows_ref, gain_ref, gate_ref, up_ref)
    total_ref[...] = jnp.broadcast_to(total, total_ref.shape)
    for e, value in enumerate(sums):
        sums_ref[e] = value
    for copy in copies:
        copy.wait()


def second_kernel(
    place_ref, rows_ref, gain_ref, gate_ref, up_ref, total_ref, sums_ref, route_ref, act_ref
):
    total, sums = half_products(1 - place_ref[0], rows_ref, gain_ref, gate_ref, up_ref)
    total = total + total_ref[:, :1]
    inverse = lax.rsqrt(total / gain_ref.shape[1] + 1e-06)
    hidden = gate_ref.shape[2]
    for e, value in enumerate(sums):
        value = (value + sums_ref[e]) * inverse
        gate = value[:, :hidden]
        active = gate / (1.0 + jnp.exp(-gate)) * value[:, hidden:]
        active = active * route_ref[:, e : e + 1]
        act_ref[:, e * hidden : (e + 1) * hidden] = active.astype(BF)


def gate_up(place, own, other, gain, route, w_gate, w_up, down_other):
    groups, _, eight, wide = own.shape
    rows = groups * eight
    experts, model, hidden = w_gate.shape
    whole = pl.BlockSpec(memory_space=pltpu.VMEM)
    where = pl.BlockSpec(memory_space=pltpu.SMEM)
    down_rows, down_columns = down_other.shape
    total, sums, down_half = pl.pallas_call(
        first_kernel,
        in_specs=[where] + [whole] * 4 + [pl.BlockSpec(memory_space=pltpu.HBM)],
        out_specs=(whole, whole, whole),
        out_shape=(
            jax.ShapeDtypeStruct((rows, 128), F32),
            jax.ShapeDtypeStruct((experts, rows, 2 * hidden), F32),
            jax.ShapeDtypeStruct((down_rows, down_columns // 2), BF),
        ),
        scratch_shapes=[pltpu.SemaphoreType.DMA((COPIES,))],
        compiler_params=limit(12),
        name="gate_up_first",
    )(place, own, gain[None], w_gate, w_up, down_other)
    act = pl.pallas_call(
        second_kernel,
        in_specs=[where] + [whole] * 7,
        out_specs=whole,
        out_shape=jax.ShapeDtypeStruct((rows, experts * hidden), BF),
        compiler_params=limit(12),
        name="gate_up_second",
    )(place, other, gain[None], w_gate, w_up, total, sums, route)
    return act, down_half


DOWN_COLUMNS = 512


def down_kernel(
    place_ref,
    act_own_ref,
    act_other_ref,
    own_ref,
    other_ref,
    after_ref,
    out_ref,
    sum_ref,
    pack_ref,
):
    del after_ref
    core = place_ref[0]
    lanes = 128
    half = own_ref.shape[1] // 2
    act = jnp.concatenate([act_own_ref[...], act_other_ref[...]], axis=1)
    tiles = DOWN_COLUMNS // lanes
    for step in range(half // DOWN_COLUMNS):
        slot = step % 2
        at = pl.ds(pl.multiple_of(core * half + step * DOWN_COLUMNS, 512), DOWN_COLUMNS)
        other = other_ref[:, step * DOWN_COLUMNS : (step + 1) * DOWN_COLUMNS]
        weights = jnp.concatenate([own_ref[:, at], other], axis=0)
        product = jnp.dot(act, weights, preferred_element_type=F32)
        for t in range(tiles):
            sum_ref[slot, t] = product[:, t * lanes : (t + 1) * lanes]
            for j in range(2):
                piece = sum_ref[slot, t, pl.ds(j, CHIPS, stride=2), :]
                pack_ref[slot, pl.ds(2 * t + j, CHIPS, stride=2 * tiles), :] = piece
        rows = slice(step * 2 * tiles, (step + 1) * 2 * tiles)
        out_ref[:, rows, :] = pack_ref[slot].astype(BF).reshape(CHIPS, 2 * tiles, lanes)


def down(place, act_own, act_other, own, other, after):
    rows = act_own.shape[0]
    out_rows = own.shape[1] // 128
    tiles = DOWN_COLUMNS // 128
    whole = pl.BlockSpec(memory_space=pltpu.VMEM)
    return pl.pallas_call(
        down_kernel,
        in_specs=[pl.BlockSpec(memory_space=pltpu.SMEM)]
        + [whole] * 4
        + [pl.BlockSpec(memory_space=pl.ANY)],
        out_specs=whole,
        out_shape=jax.ShapeDtypeStruct((CHIPS, out_rows, 128), BF),
        scratch_shapes=[
            pltpu.VMEM((2, tiles, rows, 128), F32),
            pltpu.VMEM((2, CHIPS * 2 * tiles, 128), F32),
        ],
        compiler_params=limit(8),
        name="down",
    )(place, act_own, act_other, own, other, after)


def rows_kernel(place_ref, own_ref, other_ref, after_ref, residual_ref, rows_ref):
    del after_ref
    core = place_ref[0]
    group = place_ref[1]
    quarter = place_ref[2]
    quarters, wide = own_ref.shape[1], own_ref.shape[3]
    half = quarters * wide
    place = lax.broadcasted_iota(jnp.int32, (8, wide), 0)
    for q in range(quarters):
        cols = slice(q * wide, (q + 1) * wide)

        def row(ref, at):
            block = ref[group, q].astype(F32)
            return jnp.sum(jnp.where(place == at, block, 0.0), axis=0, keepdims=True)

        first, second = row(own_ref, 2 * quarter), row(own_ref, 2 * quarter + 1)
        rows_ref[0:1, cols] = first
        rows_ref[1:2, cols] = second
        at = pl.ds(pl.multiple_of(core * half + q * wide, 128), wide)
        residual_ref[:, at] = jnp.where(core == 0, first, second).astype(BF)
        at = pl.ds(pl.multiple_of((1 - core) * half + q * wide, 128), wide)
        residual_ref[:, at] = row(other_ref, 2 * quarter + core).astype(BF)


def take_rows(place, own, other, after):
    half = own.shape[1] * own.shape[3]
    whole = pl.BlockSpec(memory_space=pltpu.VMEM)
    return pl.pallas_call(
        rows_kernel,
        in_specs=[
            pl.BlockSpec(memory_space=pltpu.SMEM),
            whole,
            whole,
            pl.BlockSpec(memory_space=pl.ANY),
        ],
        out_specs=(whole, whole),
        out_shape=(
            jax.ShapeDtypeStruct((1, 2 * half), BF),
            jax.ShapeDtypeStruct((2, half), F32),
        ),
        compiler_params=limit(4),
        name="take_rows",
    )(place, own, other, after)


def finish_kernel(place_ref, got_ref, rows_ref, mine_ref, send_ref, sum_ref):
    core = place_ref[0]
    lanes = 128
    sum_ref[...] = jnp.sum(got_ref[...].astype(F32), axis=0)
    for tile in range(rows_ref.shape[1] // lanes):
        cols = slice(tile * lanes, (tile + 1) * lanes)
        both = rows_ref[:, cols] + sum_ref[2 * tile : 2 * tile + 2, :]
        mine_ref[:, cols] = jnp.where(core == 0, both[:1], both[1:]).astype(BF)
        send_ref[:, cols] = jnp.where(core == 0, both[1:], both[:1]).astype(BF)


def finish(place, got, rows):
    whole = pl.BlockSpec(memory_space=pltpu.VMEM)
    part = jax.ShapeDtypeStruct((1, rows.shape[1]), BF)
    return pl.pallas_call(
        finish_kernel,
        in_specs=[pl.BlockSpec(memory_space=pltpu.SMEM)] + [whole] * 2,
        out_specs=(whole, whole),
        out_shape=(part, part),
        scratch_shapes=[pltpu.VMEM(got.shape[1:], F32)],
        compiler_params=limit(4),
        name="finish",
    )(place, got, rows)


def body(
    states_in,
    queries,
    kv_cache,
    kv_new,
    lengths,
    w_uv,
    w_out,
    norm_gain,
    expert_ids,
    route_scores,
    w_gate,
    w_up,
    w_down,
):
    core = lax.axis_index("core")
    group = lax.axis_index("z") * NX + lax.axis_index("x")
    quarter = lax.axis_index("y")
    model = states_in.shape[1]
    half = model // 2
    wide = half // QUARTERS
    down_own = w_down.reshape(-1, model)
    uv_other = swap(w_uv)
    out_other = swap(w_out)
    down_other = swap(down_own)
    place = jnp.stack([core, group, quarter])

    sent = attend_and_pack(
        lengths, queries, kv_cache, kv_new, states_in, expert_ids, route_scores
    )
    got = exchange(sent)
    uv, weights = fetch_halves(place, w_uv[0], uv_other[0], w_out, out_other)
    mine, send = project_values(place, got, uv, weights)
    partial, route, my_states = out_projection(place, mine, swap(send), weights)
    partial = exchange(partial.reshape(CHIPS, 8, wide))
    attention = jnp.sum(partial.astype(F32), axis=0)
    residual_part = (my_states + attention).astype(BF)
    rows_own = exchange(jnp.broadcast_to(residual_part[None], (CHIPS, 8, wide)))
    rows_other = swap(rows_own)
    rows_own = rows_own.reshape(GROUPS, NY, 8, wide)
    rows_other = rows_other.reshape(GROUPS, NY, 8, wide)

    act, down_half = gate_up(
        place, rows_own, rows_other, norm_gain, route, w_gate, w_up, down_other
    )
    residual, chip_rows = take_rows(place, rows_own, rows_other, act)
    output = down(place, act, swap(act), down_own, down_half, chip_rows)
    mine, send = finish(place, exchange(output), chip_rows)
    got = swap(send)
    layer_out = jnp.where(
        core == 0, jnp.concatenate([mine, got], axis=1), jnp.concatenate([got, mine], axis=1)
    )
    return (residual, layer_out)


def solution(mesh):
    fine = Mesh(mesh.devices.reshape(NX, NZ, NY, 2), ALL_AXES)
    rows = P(ALL_AXES, None)
    cube = P(ALL_AXES, None, None)
    in_specs = (
        rows,
        cube,
        cube,
        rows,
        P(ALL_AXES),
        cube,
        rows,
        P(),
        rows,
        rows,
        P(("x", "z"), None, ("y", "core")),
        P(("x", "z"), None, ("y", "core")),
        P(("x", "z"), ("y", "core"), None),
    )
    return jax.shard_map(body, mesh=fine, in_specs=in_specs, out_specs=(rows, rows), check_vma=False)
```

```python
import jax
import jax.numpy as jnp
from jax import lax
from jax.experimental import pallas as pl
from jax.experimental.pallas import tpu as pltpu
from jax.sharding import Mesh, PartitionSpec as P

LAT = 512
ROPE = 64
VD = 128
NX, NZ, NY = 4, 4, 4
QUARTERS = NY
CHIPS = NX * NZ * NY
GROUPS = NX * NZ
CHIP_AXES = ("z", "x", "y")
ALL_AXES = ("x", "z", "y", "core")
SWAP = [(0, 1), (1, 0)]
BF = jnp.bfloat16
F32 = jnp.float32


def swap(value):
    return lax.ppermute(value, "core", SWAP)


def exchange(value):
    return lax.all_to_all(value, CHIP_AXES, split_axis=0, concat_axis=0, tiled=True)


def limit(mib):
    return pltpu.CompilerParams(vmem_limit_bytes=mib * 1024 * 1024)


SENT_ROWS = 24
ROUTE_ROW = 8
STATE_ROW = 9
CACHE_COPIES = 4


def attend_kernel(
    length_ref,
    query_hbm,
    cache_hbm,
    newest_hbm,
    states_hbm,
    ids_hbm,
    score_hbm,
    sent_ref,
    query_ref,
    cache_ref,
    newest_ref,
    states_ref,
    ids_ref,
    score_ref,
    latent_ref,
    pack_ref,
    done,
):
    piece = cache_hbm.shape[0] // CACHE_COPIES
    pairs = [
        (cache_hbm.at[k * piece : (k + 1) * piece], cache_ref.at[k * piece : (k + 1) * piece])
        for k in range(CACHE_COPIES)
    ]
    pairs += [(query_hbm, query_ref), (newest_hbm, newest_ref)]
    early = [(states_hbm, states_ref), (ids_hbm, ids_ref), (score_hbm, score_ref)]
    copies = [
        pltpu.make_async_copy(source, target, done.at[index])
        for index, (source, target) in enumerate(pairs + early)
    ]
    for copy in copies:
        copy.start()
    for copy in copies[len(pairs) :]:
        copy.wait()
    lanes = 128
    pieces = states_ref[...].astype(F32)
    half = pieces.shape[1] // 2
    wide = half // QUARTERS
    tiles = wide // lanes
    for y in range(NY):
        for side in range(2):
            for t in range(tiles):
                at = side * half + y * wide + t * lanes
                row = y * SENT_ROWS + STATE_ROW + side * tiles + t
                pack_ref[row : row + 1, :] = pieces[:, at : at + lanes]
        pack_ref[(y + 1) * SENT_ROWS - 1 : (y + 1) * SENT_ROWS, :] = jnp.zeros((1, lanes), F32)
    first = pack_ref[: NY * SENT_ROWS, :]
    for g in range(1, GROUPS):
        pack_ref[g * NY * SENT_ROWS : (g + 1) * NY * SENT_ROWS, :] = first

    scores = score_ref[...]
    routes = (2.5 * scores / jnp.sum(scores, axis=1, keepdims=True)).astype(BF).astype(F32)
    ids = ids_ref[...]
    per_block = 3
    chip = lax.broadcasted_iota(jnp.int32, (CHIPS, lanes), 0)
    block = chip // NY % NX * NZ + chip // (NX * NY)
    lane = lax.broadcasted_iota(jnp.int32, (CHIPS, lanes), 1)
    expert = jnp.where(lane < per_block, block * per_block + lane, -1)
    dense = jnp.zeros((CHIPS, lanes), F32)
    for k in range(ids.shape[1]):
        dense = dense + jnp.where(expert == ids[:, k : k + 1], routes[:, k : k + 1], 0.0)
    pack_ref[pl.ds(ROUTE_ROW, CHIPS, stride=SENT_ROWS), :] = dense

    for copy in copies[: len(pairs)]:
        copy.wait()
    heads = query_ref.shape[1]
    positions = cache_ref.shape[1]
    softmax_scale = (VD + ROPE) ** (-0.5)
    contract_first = (((0,), (0,)), ((), ()))
    query = query_ref[...]
    cached = lax.dot_general(query, cache_ref[...], contract_first, preferred_element_type=F32)
    cached = cached * softmax_scale
    newest = newest_ref[...]
    newest_rows = jnp.broadcast_to(newest, (8, newest.shape[1]))
    own_score = lax.dot_general(
        query, newest_rows, (((0,), (1,)), ((), ())), preferred_element_type=F32
    )[:, :1]
    own_score = own_score * softmax_scale
    visible = lax.broadcasted_iota(jnp.int32, (heads, positions), 1) < length_ref[0]
    cached = jnp.where(visible, cached, -1e30)
    highest = jnp.maximum(jnp.max(cached, axis=1, keepdims=True), own_score)
    weights = jnp.where(visible, jnp.exp(cached - highest), 0.0)
    weight_own = jnp.exp(own_score - highest)
    denominator = jnp.sum(weights, axis=1, keepdims=True) + weight_own
    probs = (weights / denominator).astype(BF)
    prob_own = (weight_own / denominator).astype(BF).astype(F32)
    blended = lax.dot_general(
        probs, cache_ref[:LAT, :], (((1,), (1,)), ((), ())), preferred_element_type=F32
    )
    blended = blended + prob_own * newest[:, :LAT].astype(F32)
    for t in range(LAT // lanes):
        latent_ref[t] = blended[:, t * lanes : (t + 1) * lanes]

    for x in range(NX):
        for z in range(NZ):
            head = 2 * (x * NZ + z) * NY
            row = (z * NX + x) * NY * SENT_ROWS
            for t in range(LAT // lanes):
                for j in range(2):
                    piece = latent_ref[t, pl.ds(head + j, NY, stride=2), :]
                    pack_ref[pl.ds(row + 2 * t + j, NY, stride=SENT_ROWS), :] = piece
    sent_ref[...] = pack_ref[...].astype(BF).reshape(sent_ref.shape)


def attend_and_pack(lengths, queries, kv_cache, kv_new, states_in, expert_ids, route_scores):
    whole = pl.BlockSpec(memory_space=pltpu.VMEM)
    inputs = (queries[0].T, kv_cache[0].T, kv_new, states_in, expert_ids, route_scores)
    return pl.pallas_call(
        attend_kernel,
        in_specs=[pl.BlockSpec(memory_space=pltpu.SMEM)]
        + [pl.BlockSpec(memory_space=pltpu.HBM)] * len(inputs),
        out_specs=whole,
        out_shape=jax.ShapeDtypeStruct((CHIPS, SENT_ROWS, 128), BF),
        scratch_shapes=[pltpu.VMEM(value.shape, value.dtype) for value in inputs]
        + [
            pltpu.VMEM((LAT // 128, queries.shape[1], 128), F32),
            pltpu.VMEM((CHIPS * SENT_ROWS, 128), F32),
            pltpu.SemaphoreType.DMA((len(inputs) + CACHE_COPIES - 1,)),
        ],
        compiler_params=limit(62),
        name="attend",
    )(lengths, *inputs)


VALUE_ROWS = 3 * CHIPS + 32


def value_kernel(place_ref, got_ref, uv_ref, after_ref, mine_ref, send_ref, rows_ref, state_ref):
    del after_ref
    core = place_ref[0]
    group = place_ref[1]
    lanes = 128
    rows_ref[...] = got_ref[...].astype(F32).reshape(rows_ref.shape)

    def latent(j):
        pieces = [
            rows_ref[pl.ds(2 * t + j, CHIPS, stride=SENT_ROWS), :].astype(BF) for t in range(LAT // lanes)
        ]
        return jnp.concatenate(pieces, axis=1)

    first, second = latent(0), latent(1)
    latent_own = jnp.where(core == 0, first, second)
    latent_other = jnp.where(core == 0, second, first)
    value_own = jnp.dot(latent_own, uv_ref[0], preferred_element_type=F32).astype(BF)
    value_other = jnp.dot(latent_other, uv_ref[1], preferred_element_type=F32).astype(BF)
    routes = rows_ref[pl.ds(ROUTE_ROW, CHIPS, stride=SENT_ROWS), :].astype(BF)
    base = pl.multiple_of(group * (NY * SENT_ROWS), 8)
    tiles = 7
    for side in range(2):
        state_ref[side] = jnp.zeros(state_ref.shape[1:], F32)
    for y in range(NY):
        source = rows_ref[pl.ds(base + y * SENT_ROWS, SENT_ROWS), :]
        for side in range(2):
            at = STATE_ROW + side * tiles
            state_ref[side, 8 * y : 8 * y + tiles, :] = source[at : at + tiles, :]
    low, high = state_ref[0], state_ref[1]
    for ref, a, b in ((mine_ref, value_own, value_other), (send_ref, value_other, value_own)):
        ref[:CHIPS, :] = a
        ref[CHIPS : 2 * CHIPS, :] = b
        ref[2 * CHIPS : 3 * CHIPS, :] = routes
    mine_ref[3 * CHIPS :, :] = jnp.where(core == 0, low, high).astype(BF)
    send_ref[3 * CHIPS :, :] = jnp.where(core == 0, high, low).astype(BF)


def project_values(place, got, uv, after):
    whole = pl.BlockSpec(memory_space=pltpu.VMEM)
    out = jax.ShapeDtypeStruct((VALUE_ROWS, 128), BF)
    return pl.pallas_call(
        value_kernel,
        in_specs=[
            pl.BlockSpec(memory_space=pltpu.SMEM),
            whole,
            whole,
            pl.BlockSpec(memory_space=pl.ANY),
        ],
        out_specs=(whole, whole),
        out_shape=(out, out),
        scratch_shapes=[
            pltpu.VMEM((CHIPS * SENT_ROWS, 128), F32),
            pltpu.VMEM((2, 32, 128), F32),
        ],
        compiler_params=limit(12),
        name="values",
    )(place, got, uv, after)


def fetch_kernel(
    place_ref,
    uv_own_hbm,
    uv_other_hbm,
    own_hbm,
    other_hbm,
    uv_ref,
    weights_ref,
    done,
):
    heads = own_hbm.shape[0]
    half = weights_ref.shape[1]
    columns = pl.ds(pl.multiple_of(place_ref[0] * half, 128), half)
    copies = [
        pltpu.make_async_copy(source, target, done.at[index])
        for index, (source, target) in enumerate(
            (
                (uv_own_hbm, uv_ref.at[0]),
                (uv_other_hbm, uv_ref.at[1]),
                (own_hbm.at[:, columns], weights_ref.at[:heads]),
                (other_hbm.at[:, columns], weights_ref.at[heads:]),
            )
        )
    ]
    for copy in copies:
        copy.start()
    for copy in copies:
        copy.wait()


def fetch_halves(place, uv_own, uv_other, own, other):
    whole = pl.BlockSpec(memory_space=pltpu.VMEM)
    return pl.pallas_call(
        fetch_kernel,
        in_specs=[pl.BlockSpec(memory_space=pltpu.SMEM)]
        + [pl.BlockSpec(memory_space=pl.ANY)] * 4,
        out_specs=(whole, whole),
        out_shape=(
            jax.ShapeDtypeStruct((2,) + uv_own.shape, BF),
            jax.ShapeDtypeStruct((2 * own.shape[0], own.shape[1] // 2), BF),
        ),
        scratch_shapes=[pltpu.SemaphoreType.DMA((4,))],
        compiler_params=limit(4),
        name="fetch",
    )(place, uv_own, uv_other, own, other)


def out_kernel(
    place_ref, mine_ref, got_ref, weights_ref, out_ref, route_ref, states_ref, rows_ref, values_ref
):
    core = place_ref[0]
    lanes = 128
    mine = mine_ref[...].astype(F32)
    got = got_ref[...].astype(F32)
    even = jnp.where(core == 0, mine, got)
    odd = jnp.where(core == 0, got, mine)
    for part in range(3):
        rows = slice(part * CHIPS, (part + 1) * CHIPS)
        rows_ref[part, pl.ds(0, CHIPS, stride=2), :] = even[rows]
        rows_ref[part, pl.ds(1, CHIPS, stride=2), :] = odd[rows]
        if part < 2:
            values_ref[:, part * lanes : (part + 1) * lanes] = rows_ref[part].astype(BF)
        else:
            route_ref[...] = rows_ref[part]
    wide = states_ref.shape[1]
    for q in range(QUARTERS):
        for t in range(wide // lanes):
            at = 3 * CHIPS + 8 * q + t
            cols = slice(t * lanes, (t + 1) * lanes)
            states_ref[2 * q : 2 * q + 1, cols] = even[at : at + 1, :]
            states_ref[2 * q + 1 : 2 * q + 2, cols] = odd[at : at + 1, :]
    values = values_ref[...]
    groups = out_ref.shape[0]
    for q in range(QUARTERS):
        product = jnp.dot(values, weights_ref[:, q * wide : (q + 1) * wide], preferred_element_type=F32)
        out_ref[:, q] = product.astype(BF).reshape(groups, 8, wide)


def out_projection(place, mine, got, weights):
    rows = 2 * CHIPS
    wide = weights.shape[1] // QUARTERS
    whole = pl.BlockSpec(memory_space=pltpu.VMEM)
    return pl.pallas_call(
        out_kernel,
        in_specs=[pl.BlockSpec(memory_space=pltpu.SMEM), whole, whole, whole],
        out_specs=(whole, whole, whole),
        out_shape=(
            jax.ShapeDtypeStruct((rows // 8, QUARTERS, 8, wide), BF),
            jax.ShapeDtypeStruct((rows, 128), F32),
            jax.ShapeDtypeStruct((8, wide), F32),
        ),
        scratch_shapes=[pltpu.VMEM((3, rows, 128), F32), pltpu.VMEM((rows, 2 * VD), BF)],
        compiler_params=limit(12),
        name="out_projection",
    )(place, mine, got, weights)


def half_products(half, rows_ref, gain_ref, gate_ref, up_ref):
    groups, quarters, eight, wide = rows_ref.shape
    rows = groups * eight
    experts = gate_ref.shape[0]
    total = jnp.zeros((rows, 1), F32)
    sums = [None] * experts
    for pair in range(quarters // 2):
        pieces = [rows_ref[:, q].reshape(rows, wide) for q in (2 * pair, 2 * pair + 1)]
        piece = jnp.concatenate(pieces, axis=1).astype(F32)
        total = total + jnp.sum(piece * piece, axis=1, keepdims=True)
        at = pl.ds(pl.multiple_of(half * (quarters * wide) + pair * (2 * wide), 256), 2 * wide)
        scaled = (piece * gain_ref[:, at]).astype(BF)
        for e in range(experts):
            weights = jnp.concatenate([gate_ref[e, at, :], up_ref[e, at, :]], axis=1)
            product = jnp.dot(scaled, weights, preferred_element_type=F32)
            sums[e] = product if sums[e] is None else sums[e] + product
    return total, sums


def first_kernel(place_ref, rows_ref, gain_ref, gate_ref, up_ref, total_ref, sums_ref):
    total, sums = half_products(place_ref[0], rows_ref, gain_ref, gate_ref, up_ref)
    total_ref[...] = jnp.broadcast_to(total, total_ref.shape)
    for e, value in enumerate(sums):
        sums_ref[e] = value


def second_kernel(
    place_ref, rows_ref, gain_ref, gate_ref, up_ref, total_ref, sums_ref, route_ref, act_ref
):
    total, sums = half_products(1 - place_ref[0], rows_ref, gain_ref, gate_ref, up_ref)
    total = total + total_ref[:, :1]
    inverse = lax.rsqrt(total / gain_ref.shape[1] + 1e-06)
    hidden = gate_ref.shape[2]
    for e, value in enumerate(sums):
        value = (value + sums_ref[e]) * inverse
        gate = value[:, :hidden]
        active = gate / (1.0 + jnp.exp(-gate)) * value[:, hidden:]
        active = active * route_ref[:, e : e + 1]
        act_ref[:, e * hidden : (e + 1) * hidden] = active.astype(BF)


def gate_up(place, own, other, gain, route, w_gate, w_up):
    groups, _, eight, wide = own.shape
    rows = groups * eight
    experts, model, hidden = w_gate.shape
    whole = pl.BlockSpec(memory_space=pltpu.VMEM)
    where = pl.BlockSpec(memory_space=pltpu.SMEM)
    total, sums = pl.pallas_call(
        first_kernel,
        in_specs=[where] + [whole] * 4,
        out_specs=(whole, whole),
        out_shape=(
            jax.ShapeDtypeStruct((rows, 128), F32),
            jax.ShapeDtypeStruct((experts, rows, 2 * hidden), F32),
        ),
        compiler_params=limit(12),
        name="gate_up_first",
    )(place, own, gain[None], w_gate, w_up)
    act = pl.pallas_call(
        second_kernel,
        in_specs=[where] + [whole] * 7,
        out_specs=whole,
        out_shape=jax.ShapeDtypeStruct((rows, experts * hidden), BF),
        compiler_params=limit(12),
        name="gate_up_second",
    )(place, other, gain[None], w_gate, w_up, total, sums, route)
    return act


DOWN_COLUMNS = 512


def down_kernel(
    place_ref,
    act_own_ref,
    act_other_ref,
    own_ref,
    other_refs,
    after_ref,
    out_ref,
    sum_ref,
    pack_ref,
):
    del after_ref
    core = place_ref[0]
    lanes = 128
    half = own_ref.shape[1] // 2
    act = jnp.concatenate([act_own_ref[...], act_other_ref[...]], axis=1)
    tiles = DOWN_COLUMNS // lanes
    for step in range(half // DOWN_COLUMNS):
        slot = step % 2
        at = pl.ds(pl.multiple_of(core * half + step * DOWN_COLUMNS, 512), DOWN_COLUMNS)
        weights = jnp.concatenate([own_ref[:, at]] + [ref[:, at] for ref in other_refs], axis=0)
        product = jnp.dot(act, weights, preferred_element_type=F32)
        for t in range(tiles):
            sum_ref[slot, t] = product[:, t * lanes : (t + 1) * lanes]
            for j in range(2):
                piece = sum_ref[slot, t, pl.ds(j, CHIPS, stride=2), :]
                pack_ref[slot, pl.ds(2 * t + j, CHIPS, stride=2 * tiles), :] = piece
        rows = slice(step * 2 * tiles, (step + 1) * 2 * tiles)
        out_ref[:, rows, :] = pack_ref[slot].astype(BF).reshape(CHIPS, 2 * tiles, lanes)


def down(place, act_own, act_other, own, other, after):
    rows = act_own.shape[0]
    out_rows = own.shape[1] // 128
    tiles = DOWN_COLUMNS // 128
    whole = pl.BlockSpec(memory_space=pltpu.VMEM)
    return pl.pallas_call(
        down_kernel,
        in_specs=[
            pl.BlockSpec(memory_space=pltpu.SMEM),
            whole,
            whole,
            whole,
            [whole] * len(other),
            pl.BlockSpec(memory_space=pl.ANY),
        ],
        out_specs=whole,
        out_shape=jax.ShapeDtypeStruct((CHIPS, out_rows, 128), BF),
        scratch_shapes=[
            pltpu.VMEM((2, tiles, rows, 128), F32),
            pltpu.VMEM((2, CHIPS * 2 * tiles, 128), F32),
        ],
        compiler_params=limit(8),
        name="down",
    )(place, act_own, act_other, own, other, after)


def rows_kernel(place_ref, own_ref, other_ref, after_ref, residual_ref, rows_ref):
    del after_ref
    core = place_ref[0]
    group = place_ref[1]
    quarter = place_ref[2]
    quarters, wide = own_ref.shape[1], own_ref.shape[3]
    half = quarters * wide
    place = lax.broadcasted_iota(jnp.int32, (8, wide), 0)
    for q in range(quarters):
        cols = slice(q * wide, (q + 1) * wide)

        def row(ref, at):
            block = ref[group, q].astype(F32)
            return jnp.sum(jnp.where(place == at, block, 0.0), axis=0, keepdims=True)

        first, second = row(own_ref, 2 * quarter), row(own_ref, 2 * quarter + 1)
        rows_ref[0:1, cols] = first
        rows_ref[1:2, cols] = second
        at = pl.ds(pl.multiple_of(core * half + q * wide, 128), wide)
        residual_ref[:, at] = jnp.where(core == 0, first, second).astype(BF)
        at = pl.ds(pl.multiple_of((1 - core) * half + q * wide, 128), wide)
        residual_ref[:, at] = row(other_ref, 2 * quarter + core).astype(BF)


def take_rows(place, own, other, after):
    half = own.shape[1] * own.shape[3]
    whole = pl.BlockSpec(memory_space=pltpu.VMEM)
    return pl.pallas_call(
        rows_kernel,
        in_specs=[
            pl.BlockSpec(memory_space=pltpu.SMEM),
            whole,
            whole,
            pl.BlockSpec(memory_space=pl.ANY),
        ],
        out_specs=(whole, whole),
        out_shape=(
            jax.ShapeDtypeStruct((1, 2 * half), BF),
            jax.ShapeDtypeStruct((2, half), F32),
        ),
        compiler_params=limit(4),
        name="take_rows",
    )(place, own, other, after)


def finish_kernel(place_ref, got_ref, rows_ref, mine_ref, send_ref, sum_ref):
    core = place_ref[0]
    lanes = 128
    sum_ref[...] = jnp.sum(got_ref[...].astype(F32), axis=0)
    for tile in range(rows_ref.shape[1] // lanes):
        cols = slice(tile * lanes, (tile + 1) * lanes)
        both = rows_ref[:, cols] + sum_ref[2 * tile : 2 * tile + 2, :]
        mine_ref[:, cols] = jnp.where(core == 0, both[:1], both[1:]).astype(BF)
        send_ref[:, cols] = jnp.where(core == 0, both[1:], both[:1]).astype(BF)


def finish(place, got, rows):
    whole = pl.BlockSpec(memory_space=pltpu.VMEM)
    part = jax.ShapeDtypeStruct((1, rows.shape[1]), BF)
    return pl.pallas_call(
        finish_kernel,
        in_specs=[pl.BlockSpec(memory_space=pltpu.SMEM)] + [whole] * 2,
        out_specs=(whole, whole),
        out_shape=(part, part),
        scratch_shapes=[pltpu.VMEM(got.shape[1:], F32)],
        compiler_params=limit(4),
        name="finish",
    )(place, got, rows)


def body(
    states_in,
    queries,
    kv_cache,
    kv_new,
    lengths,
    w_uv,
    w_out,
    norm_gain,
    expert_ids,
    route_scores,
    w_gate,
    w_up,
    w_down,
):
    core = lax.axis_index("core")
    group = lax.axis_index("z") * NX + lax.axis_index("x")
    quarter = lax.axis_index("y")
    model = states_in.shape[1]
    half = model // 2
    wide = half // QUARTERS
    down_own = w_down.reshape(-1, model)
    uv_other = swap(w_uv)
    out_other = swap(w_out)
    place = jnp.stack([core, group, quarter])

    sent = attend_and_pack(
        lengths, queries, kv_cache, kv_new, states_in, expert_ids, route_scores
    )
    got = exchange(sent)
    uv, weights = fetch_halves(place, w_uv[0], uv_other[0], w_out, out_other)
    mine, send = project_values(place, got, uv, weights)
    partial, route, my_states = out_projection(place, mine, swap(send), weights)
    partial, down_sent = lax.optimization_barrier((partial, down_own))
    down_other = [swap(down_sent)]
    partial = exchange(partial.reshape(CHIPS, 8, wide))
    attention = jnp.sum(partial.astype(F32), axis=0)
    residual_part = (my_states + attention).astype(BF)
    rows_own = exchange(jnp.broadcast_to(residual_part[None], (CHIPS, 8, wide)))
    rows_other = swap(rows_own)
    rows_own = rows_own.reshape(GROUPS, NY, 8, wide)
    rows_other = rows_other.reshape(GROUPS, NY, 8, wide)

    act = gate_up(place, rows_own, rows_other, norm_gain, route, w_gate, w_up)
    residual, chip_rows = take_rows(place, rows_own, rows_other, act)
    output = down(place, act, swap(act), down_own, down_other, chip_rows)
    mine, send = finish(place, exchange(output), chip_rows)
    got = swap(send)
    layer_out = jnp.where(
        core == 0, jnp.concatenate([mine, got], axis=1), jnp.concatenate([got, mine], axis=1)
    )
    return (residual, layer_out)


def solution(mesh):
    fine = Mesh(mesh.devices.reshape(NX, NZ, NY, 2), ALL_AXES)
    rows = P(ALL_AXES, None)
    cube = P(ALL_AXES, None, None)
    in_specs = (
        rows,
        cube,
        cube,
        rows,
        P(ALL_AXES),
        cube,
        rows,
        P(),
        rows,
        rows,
        P(("x", "z"), None, ("y", "core")),
        P(("x", "z"), None, ("y", "core")),
        P(("x", "z"), ("y", "core"), None),
    )
    return jax.shard_map(body, mesh=fine, in_specs=in_specs, out_specs=(rows, rows), check_vma=False)
```

```python
import jax
import jax.numpy as jnp
from jax import lax
from jax.experimental import pallas as pl
from jax.experimental.pallas import tpu as pltpu
from jax.sharding import Mesh, PartitionSpec as P

LAT = 512
ROPE = 64
VD = 128
NX, NZ, NY = 4, 4, 4
QUARTERS = NY
CHIPS = NX * NZ * NY
GROUPS = NX * NZ
CHIP_AXES = ("z", "x", "y")
ALL_AXES = ("x", "z", "y", "core")
SWAP = [(0, 1), (1, 0)]
BF = jnp.bfloat16
F32 = jnp.float32


def swap(value):
    return lax.ppermute(value, "core", SWAP)


def exchange(value):
    return lax.all_to_all(value, CHIP_AXES, split_axis=0, concat_axis=0, tiled=True)


def limit(mib):
    return pltpu.CompilerParams(vmem_limit_bytes=mib * 1024 * 1024)


SENT_ROWS = 24
ROUTE_ROW = 8
STATE_ROW = 9
CACHE_COPIES = 4


def attend_kernel(
    length_ref,
    query_hbm,
    cache_hbm,
    newest_hbm,
    states_hbm,
    ids_hbm,
    score_hbm,
    sent_ref,
    query_ref,
    cache_ref,
    newest_ref,
    states_ref,
    ids_ref,
    score_ref,
    latent_ref,
    pack_ref,
    done,
):
    piece = cache_hbm.shape[0] // CACHE_COPIES
    pairs = [
        (cache_hbm.at[k * piece : (k + 1) * piece], cache_ref.at[k * piece : (k + 1) * piece])
        for k in range(CACHE_COPIES)
    ]
    pairs += [(query_hbm, query_ref), (newest_hbm, newest_ref)]
    early = [(states_hbm, states_ref), (ids_hbm, ids_ref), (score_hbm, score_ref)]
    copies = [
        pltpu.make_async_copy(source, target, done.at[index])
        for index, (source, target) in enumerate(pairs + early)
    ]
    for copy in copies:
        copy.start()
    for copy in copies[len(pairs) :]:
        copy.wait()
    lanes = 128
    pieces = states_ref[...].astype(F32)
    half = pieces.shape[1] // 2
    wide = half // QUARTERS
    tiles = wide // lanes
    for y in range(NY):
        for side in range(2):
            for t in range(tiles):
                at = side * half + y * wide + t * lanes
                row = y * SENT_ROWS + STATE_ROW + side * tiles + t
                pack_ref[row : row + 1, :] = pieces[:, at : at + lanes]
        pack_ref[(y + 1) * SENT_ROWS - 1 : (y + 1) * SENT_ROWS, :] = jnp.zeros((1, lanes), F32)
    first = pack_ref[: NY * SENT_ROWS, :]
    for g in range(1, GROUPS):
        pack_ref[g * NY * SENT_ROWS : (g + 1) * NY * SENT_ROWS, :] = first

    scores = score_ref[...]
    routes = (2.5 * scores / jnp.sum(scores, axis=1, keepdims=True)).astype(BF).astype(F32)
    ids = ids_ref[...]
    per_block = 3
    chip = lax.broadcasted_iota(jnp.int32, (CHIPS, lanes), 0)
    block = chip // NY % NX * NZ + chip // (NX * NY)
    lane = lax.broadcasted_iota(jnp.int32, (CHIPS, lanes), 1)
    expert = jnp.where(lane < per_block, block * per_block + lane, -1)
    dense = jnp.zeros((CHIPS, lanes), F32)
    for k in range(ids.shape[1]):
        dense = dense + jnp.where(expert == ids[:, k : k + 1], routes[:, k : k + 1], 0.0)
    pack_ref[pl.ds(ROUTE_ROW, CHIPS, stride=SENT_ROWS), :] = dense

    for copy in copies[: len(pairs)]:
        copy.wait()
    heads = query_ref.shape[1]
    positions = cache_ref.shape[1]
    softmax_scale = (VD + ROPE) ** (-0.5)
    contract_first = (((0,), (0,)), ((), ()))
    query = query_ref[...]
    cached = lax.dot_general(query, cache_ref[...], contract_first, preferred_element_type=F32)
    cached = cached * softmax_scale
    newest = newest_ref[...]
    newest_rows = jnp.broadcast_to(newest, (8, newest.shape[1]))
    own_score = lax.dot_general(
        query, newest_rows, (((0,), (1,)), ((), ())), preferred_element_type=F32
    )[:, :1]
    own_score = own_score * softmax_scale
    visible = lax.broadcasted_iota(jnp.int32, (heads, positions), 1) < length_ref[0]
    cached = jnp.where(visible, cached, -1e30)
    highest = jnp.maximum(jnp.max(cached, axis=1, keepdims=True), own_score)
    weights = jnp.where(visible, jnp.exp(cached - highest), 0.0)
    weight_own = jnp.exp(own_score - highest)
    denominator = jnp.sum(weights, axis=1, keepdims=True) + weight_own
    probs = (weights / denominator).astype(BF)
    prob_own = (weight_own / denominator).astype(BF).astype(F32)
    blended = lax.dot_general(
        probs, cache_ref[:LAT, :], (((1,), (1,)), ((), ())), preferred_element_type=F32
    )
    blended = blended + prob_own * newest[:, :LAT].astype(F32)
    for t in range(LAT // lanes):
        latent_ref[t] = blended[:, t * lanes : (t + 1) * lanes]

    for x in range(NX):
        for z in range(NZ):
            head = 2 * (x * NZ + z) * NY
            row = (z * NX + x) * NY * SENT_ROWS
            for t in range(LAT // lanes):
                for j in range(2):
                    piece = latent_ref[t, pl.ds(head + j, NY, stride=2), :]
                    pack_ref[pl.ds(row + 2 * t + j, NY, stride=SENT_ROWS), :] = piece
    sent_ref[...] = pack_ref[...].astype(BF).reshape(sent_ref.shape)


def attend_and_pack(lengths, queries, kv_cache, kv_new, states_in, expert_ids, route_scores):
    whole = pl.BlockSpec(memory_space=pltpu.VMEM)
    inputs = (queries[0].T, kv_cache[0].T, kv_new, states_in, expert_ids, route_scores)
    return pl.pallas_call(
        attend_kernel,
        in_specs=[pl.BlockSpec(memory_space=pltpu.SMEM)]
        + [pl.BlockSpec(memory_space=pltpu.HBM)] * len(inputs),
        out_specs=whole,
        out_shape=jax.ShapeDtypeStruct((CHIPS, SENT_ROWS, 128), BF),
        scratch_shapes=[pltpu.VMEM(value.shape, value.dtype) for value in inputs]
        + [
            pltpu.VMEM((LAT // 128, queries.shape[1], 128), F32),
            pltpu.VMEM((CHIPS * SENT_ROWS, 128), F32),
            pltpu.SemaphoreType.DMA((len(inputs) + CACHE_COPIES - 1,)),
        ],
        compiler_params=limit(62),
        name="attend",
    )(lengths, *inputs)


VALUE_ROWS = 3 * CHIPS + 32


def value_kernel(place_ref, got_ref, uv_ref, after_ref, mine_ref, send_ref, rows_ref, state_ref):
    del after_ref
    core = place_ref[0]
    group = place_ref[1]
    lanes = 128
    rows_ref[...] = got_ref[...].astype(F32).reshape(rows_ref.shape)

    def latent(j):
        pieces = [
            rows_ref[pl.ds(2 * t + j, CHIPS, stride=SENT_ROWS), :].astype(BF) for t in range(LAT // lanes)
        ]
        return jnp.concatenate(pieces, axis=1)

    first, second = latent(0), latent(1)
    latent_own = jnp.where(core == 0, first, second)
    latent_other = jnp.where(core == 0, second, first)
    value_own = jnp.dot(latent_own, uv_ref[0], preferred_element_type=F32).astype(BF)
    value_other = jnp.dot(latent_other, uv_ref[1], preferred_element_type=F32).astype(BF)
    routes = rows_ref[pl.ds(ROUTE_ROW, CHIPS, stride=SENT_ROWS), :].astype(BF)
    base = pl.multiple_of(group * (NY * SENT_ROWS), 8)
    tiles = 7
    for side in range(2):
        state_ref[side] = jnp.zeros(state_ref.shape[1:], F32)
    for y in range(NY):
        source = rows_ref[pl.ds(base + y * SENT_ROWS, SENT_ROWS), :]
        for side in range(2):
            at = STATE_ROW + side * tiles
            state_ref[side, 8 * y : 8 * y + tiles, :] = source[at : at + tiles, :]
    low, high = state_ref[0], state_ref[1]
    for ref, a, b in ((mine_ref, value_own, value_other), (send_ref, value_other, value_own)):
        ref[:CHIPS, :] = a
        ref[CHIPS : 2 * CHIPS, :] = b
        ref[2 * CHIPS : 3 * CHIPS, :] = routes
    mine_ref[3 * CHIPS :, :] = jnp.where(core == 0, low, high).astype(BF)
    send_ref[3 * CHIPS :, :] = jnp.where(core == 0, high, low).astype(BF)


def project_values(place, got, uv, after):
    whole = pl.BlockSpec(memory_space=pltpu.VMEM)
    out = jax.ShapeDtypeStruct((VALUE_ROWS, 128), BF)
    return pl.pallas_call(
        value_kernel,
        in_specs=[
            pl.BlockSpec(memory_space=pltpu.SMEM),
            whole,
            whole,
            pl.BlockSpec(memory_space=pl.ANY),
        ],
        out_specs=(whole, whole),
        out_shape=(out, out),
        scratch_shapes=[
            pltpu.VMEM((CHIPS * SENT_ROWS, 128), F32),
            pltpu.VMEM((2, 32, 128), F32),
        ],
        compiler_params=limit(12),
        name="values",
    )(place, got, uv, after)


def fetch_kernel(
    place_ref,
    uv_own_hbm,
    uv_other_hbm,
    own_hbm,
    other_hbm,
    uv_ref,
    weights_ref,
    done,
):
    heads = own_hbm.shape[0]
    half = weights_ref.shape[1]
    columns = pl.ds(pl.multiple_of(place_ref[0] * half, 128), half)
    copies = [
        pltpu.make_async_copy(source, target, done.at[index])
        for index, (source, target) in enumerate(
            (
                (uv_own_hbm, uv_ref.at[0]),
                (uv_other_hbm, uv_ref.at[1]),
                (own_hbm.at[:, columns], weights_ref.at[:heads]),
                (other_hbm.at[:, columns], weights_ref.at[heads:]),
            )
        )
    ]
    for copy in copies:
        copy.start()
    for copy in copies:
        copy.wait()


def fetch_halves(place, uv_own, uv_other, own, other):
    whole = pl.BlockSpec(memory_space=pltpu.VMEM)
    return pl.pallas_call(
        fetch_kernel,
        in_specs=[pl.BlockSpec(memory_space=pltpu.SMEM)]
        + [pl.BlockSpec(memory_space=pl.ANY)] * 4,
        out_specs=(whole, whole),
        out_shape=(
            jax.ShapeDtypeStruct((2,) + uv_own.shape, BF),
            jax.ShapeDtypeStruct((2 * own.shape[0], own.shape[1] // 2), BF),
        ),
        scratch_shapes=[pltpu.SemaphoreType.DMA((4,))],
        compiler_params=limit(4),
        name="fetch",
    )(place, uv_own, uv_other, own, other)


def out_kernel(
    place_ref, mine_ref, got_ref, weights_ref, out_ref, route_ref, states_ref, rows_ref, values_ref
):
    core = place_ref[0]
    lanes = 128
    mine = mine_ref[...].astype(F32)
    got = got_ref[...].astype(F32)
    even = jnp.where(core == 0, mine, got)
    odd = jnp.where(core == 0, got, mine)
    for part in range(3):
        rows = slice(part * CHIPS, (part + 1) * CHIPS)
        rows_ref[part, pl.ds(0, CHIPS, stride=2), :] = even[rows]
        rows_ref[part, pl.ds(1, CHIPS, stride=2), :] = odd[rows]
        if part < 2:
            values_ref[:, part * lanes : (part + 1) * lanes] = rows_ref[part].astype(BF)
        else:
            route_ref[...] = rows_ref[part]
    wide = states_ref.shape[1]
    for q in range(QUARTERS):
        for t in range(wide // lanes):
            at = 3 * CHIPS + 8 * q + t
            cols = slice(t * lanes, (t + 1) * lanes)
            states_ref[2 * q : 2 * q + 1, cols] = even[at : at + 1, :]
            states_ref[2 * q + 1 : 2 * q + 2, cols] = odd[at : at + 1, :]
    values = values_ref[...]
    groups = out_ref.shape[0]
    for q in range(QUARTERS):
        product = jnp.dot(values, weights_ref[:, q * wide : (q + 1) * wide], preferred_element_type=F32)
        out_ref[:, q] = product.astype(BF).reshape(groups, 8, wide)


def out_projection(place, mine, got, weights):
    rows = 2 * CHIPS
    wide = weights.shape[1] // QUARTERS
    whole = pl.BlockSpec(memory_space=pltpu.VMEM)
    return pl.pallas_call(
        out_kernel,
        in_specs=[pl.BlockSpec(memory_space=pltpu.SMEM), whole, whole, whole],
        out_specs=(whole, whole, whole),
        out_shape=(
            jax.ShapeDtypeStruct((rows // 8, QUARTERS, 8, wide), BF),
            jax.ShapeDtypeStruct((rows, 128), F32),
            jax.ShapeDtypeStruct((8, wide), F32),
        ),
        scratch_shapes=[pltpu.VMEM((3, rows, 128), F32), pltpu.VMEM((rows, 2 * VD), BF)],
        compiler_params=limit(12),
        name="out_projection",
    )(place, mine, got, weights)


def half_products(half, rows_ref, gain_ref, gate_ref, up_ref):
    groups, quarters, eight, wide = rows_ref.shape
    rows = groups * eight
    experts = gate_ref.shape[0]
    pieces = [rows_ref[:, q].reshape(rows, wide) for q in range(quarters)]
    piece = jnp.concatenate(pieces, axis=1).astype(F32)
    total = jnp.sum(piece * piece, axis=1, keepdims=True)
    at = pl.ds(pl.multiple_of(half * (quarters * wide), 256), quarters * wide)
    scaled = (piece * gain_ref[:, at]).astype(BF)
    sums = []
    for e in range(experts):
        weights = jnp.concatenate([gate_ref[e, at, :], up_ref[e, at, :]], axis=1)
        sums.append(jnp.dot(scaled, weights, preferred_element_type=F32))
    return total, sums


def first_kernel(place_ref, rows_ref, gain_ref, gate_ref, up_ref, total_ref, sums_ref):
    total, sums = half_products(place_ref[0], rows_ref, gain_ref, gate_ref, up_ref)
    total_ref[...] = jnp.broadcast_to(total, total_ref.shape)
    for e, value in enumerate(sums):
        sums_ref[e] = value


def second_kernel(
    place_ref, rows_ref, gain_ref, gate_ref, up_ref, total_ref, sums_ref, route_ref, act_ref
):
    total, sums = half_products(1 - place_ref[0], rows_ref, gain_ref, gate_ref, up_ref)
    total = total + total_ref[:, :1]
    inverse = lax.rsqrt(total / gain_ref.shape[1] + 1e-06)
    hidden = gate_ref.shape[2]
    for e, value in enumerate(sums):
        value = (value + sums_ref[e]) * inverse
        gate = value[:, :hidden]
        active = gate / (1.0 + jnp.exp(-gate)) * value[:, hidden:]
        active = active * route_ref[:, e : e + 1]
        act_ref[:, e * hidden : (e + 1) * hidden] = active.astype(BF)


def gate_up(place, own, other, gain, route, w_gate, w_up):
    groups, _, eight, wide = own.shape
    rows = groups * eight
    experts, model, hidden = w_gate.shape
    whole = pl.BlockSpec(memory_space=pltpu.VMEM)
    where = pl.BlockSpec(memory_space=pltpu.SMEM)
    total, sums = pl.pallas_call(
        first_kernel,
        in_specs=[where] + [whole] * 4,
        out_specs=(whole, whole),
        out_shape=(
            jax.ShapeDtypeStruct((rows, 128), F32),
            jax.ShapeDtypeStruct((experts, rows, 2 * hidden), F32),
        ),
        compiler_params=limit(12),
        name="gate_up_first",
    )(place, own, gain[None], w_gate, w_up)
    act = pl.pallas_call(
        second_kernel,
        in_specs=[where] + [whole] * 7,
        out_specs=whole,
        out_shape=jax.ShapeDtypeStruct((rows, experts * hidden), BF),
        compiler_params=limit(12),
        name="gate_up_second",
    )(place, other, gain[None], w_gate, w_up, total, sums, route)
    return act


DOWN_COLUMNS = 512


def down_kernel(
    place_ref,
    act_own_ref,
    act_other_ref,
    own_ref,
    other_refs,
    after_ref,
    out_ref,
    sum_ref,
    pack_ref,
):
    del after_ref
    core = place_ref[0]
    lanes = 128
    half = own_ref.shape[1] // 2
    act = jnp.concatenate([act_own_ref[...], act_other_ref[...]], axis=1)
    tiles = DOWN_COLUMNS // lanes
    for step in range(half // DOWN_COLUMNS):
        slot = step % 2
        at = pl.ds(pl.multiple_of(core * half + step * DOWN_COLUMNS, 512), DOWN_COLUMNS)
        weights = jnp.concatenate([own_ref[:, at]] + [ref[:, at] for ref in other_refs], axis=0)
        product = jnp.dot(act, weights, preferred_element_type=F32)
        for t in range(tiles):
            sum_ref[slot, t] = product[:, t * lanes : (t + 1) * lanes]
            for j in range(2):
                piece = sum_ref[slot, t, pl.ds(j, CHIPS, stride=2), :]
                pack_ref[slot, pl.ds(2 * t + j, CHIPS, stride=2 * tiles), :] = piece
        rows = slice(step * 2 * tiles, (step + 1) * 2 * tiles)
        out_ref[:, rows, :] = pack_ref[slot].astype(BF).reshape(CHIPS, 2 * tiles, lanes)


def down(place, act_own, act_other, own, other, after):
    rows = act_own.shape[0]
    out_rows = own.shape[1] // 128
    tiles = DOWN_COLUMNS // 128
    whole = pl.BlockSpec(memory_space=pltpu.VMEM)
    return pl.pallas_call(
        down_kernel,
        in_specs=[
            pl.BlockSpec(memory_space=pltpu.SMEM),
            whole,
            whole,
            whole,
            [whole] * len(other),
            pl.BlockSpec(memory_space=pl.ANY),
        ],
        out_specs=whole,
        out_shape=jax.ShapeDtypeStruct((CHIPS, out_rows, 128), BF),
        scratch_shapes=[
            pltpu.VMEM((2, tiles, rows, 128), F32),
            pltpu.VMEM((2, CHIPS * 2 * tiles, 128), F32),
        ],
        compiler_params=limit(8),
        name="down",
    )(place, act_own, act_other, own, other, after)


def rows_kernel(place_ref, own_ref, other_ref, after_ref, residual_ref, rows_ref):
    del after_ref
    core = place_ref[0]
    group = place_ref[1]
    quarter = place_ref[2]
    quarters, wide = own_ref.shape[1], own_ref.shape[3]
    half = quarters * wide
    place = lax.broadcasted_iota(jnp.int32, (8, wide), 0)
    for q in range(quarters):
        cols = slice(q * wide, (q + 1) * wide)

        def row(ref, at):
            block = ref[group, q].astype(F32)
            return jnp.sum(jnp.where(place == at, block, 0.0), axis=0, keepdims=True)

        first, second = row(own_ref, 2 * quarter), row(own_ref, 2 * quarter + 1)
        rows_ref[0:1, cols] = first
        rows_ref[1:2, cols] = second
        at = pl.ds(pl.multiple_of(core * half + q * wide, 128), wide)
        residual_ref[:, at] = jnp.where(core == 0, first, second).astype(BF)
        at = pl.ds(pl.multiple_of((1 - core) * half + q * wide, 128), wide)
        residual_ref[:, at] = row(other_ref, 2 * quarter + core).astype(BF)


def take_rows(place, own, other, after):
    half = own.shape[1] * own.shape[3]
    whole = pl.BlockSpec(memory_space=pltpu.VMEM)
    return pl.pallas_call(
        rows_kernel,
        in_specs=[
            pl.BlockSpec(memory_space=pltpu.SMEM),
            whole,
            whole,
            pl.BlockSpec(memory_space=pl.ANY),
        ],
        out_specs=(whole, whole),
        out_shape=(
            jax.ShapeDtypeStruct((1, 2 * half), BF),
            jax.ShapeDtypeStruct((2, half), F32),
        ),
        compiler_params=limit(4),
        name="take_rows",
    )(place, own, other, after)


def finish_kernel(place_ref, got_ref, rows_ref, mine_ref, send_ref, sum_ref):
    core = place_ref[0]
    lanes = 128
    sum_ref[...] = jnp.sum(got_ref[...].astype(F32), axis=0)
    for tile in range(rows_ref.shape[1] // lanes):
        cols = slice(tile * lanes, (tile + 1) * lanes)
        both = rows_ref[:, cols] + sum_ref[2 * tile : 2 * tile + 2, :]
        mine_ref[:, cols] = jnp.where(core == 0, both[:1], both[1:]).astype(BF)
        send_ref[:, cols] = jnp.where(core == 0, both[1:], both[:1]).astype(BF)


def finish(place, got, rows):
    whole = pl.BlockSpec(memory_space=pltpu.VMEM)
    part = jax.ShapeDtypeStruct((1, rows.shape[1]), BF)
    return pl.pallas_call(
        finish_kernel,
        in_specs=[pl.BlockSpec(memory_space=pltpu.SMEM)] + [whole] * 2,
        out_specs=(whole, whole),
        out_shape=(part, part),
        scratch_shapes=[pltpu.VMEM(got.shape[1:], F32)],
        compiler_params=limit(4),
        name="finish",
    )(place, got, rows)


def body(
    states_in,
    queries,
    kv_cache,
    kv_new,
    lengths,
    w_uv,
    w_out,
    norm_gain,
    expert_ids,
    route_scores,
    w_gate,
    w_up,
    w_down,
):
    core = lax.axis_index("core")
    group = lax.axis_index("z") * NX + lax.axis_index("x")
    quarter = lax.axis_index("y")
    model = states_in.shape[1]
    half = model // 2
    wide = half // QUARTERS
    down_own = w_down.reshape(-1, model)
    uv_other = swap(w_uv)
    out_other = swap(w_out)
    place = jnp.stack([core, group, quarter])

    sent = attend_and_pack(
        lengths, queries, kv_cache, kv_new, states_in, expert_ids, route_scores
    )
    got = exchange(sent)
    uv, weights = fetch_halves(place, w_uv[0], uv_other[0], w_out, out_other)
    mine, send = project_values(place, got, uv, weights)
    partial, route, my_states = out_projection(place, mine, swap(send), weights)
    partial, down_sent = lax.optimization_barrier((partial, down_own))
    down_other = [swap(down_sent)]
    partial = exchange(partial.reshape(CHIPS, 8, wide))
    attention = jnp.sum(partial.astype(F32), axis=0)
    residual_part = (my_states + attention).astype(BF)
    rows_own = exchange(jnp.broadcast_to(residual_part[None], (CHIPS, 8, wide)))
    rows_other = swap(rows_own)
    rows_own = rows_own.reshape(GROUPS, NY, 8, wide)
    rows_other = rows_other.reshape(GROUPS, NY, 8, wide)

    act = gate_up(place, rows_own, rows_other, norm_gain, route, w_gate, w_up)
    residual, chip_rows = take_rows(place, rows_own, rows_other, act)
    output = down(place, act, swap(act), down_own, down_other, chip_rows)
    mine, send = finish(place, exchange(output), chip_rows)
    got = swap(send)
    layer_out = jnp.where(
        core == 0, jnp.concatenate([mine, got], axis=1), jnp.concatenate([got, mine], axis=1)
    )
    return (residual, layer_out)


def solution(mesh):
    fine = Mesh(mesh.devices.reshape(NX, NZ, NY, 2), ALL_AXES)
    rows = P(ALL_AXES, None)
    cube = P(ALL_AXES, None, None)
    in_specs = (
        rows,
        cube,
        cube,
        rows,
        P(ALL_AXES),
        cube,
        rows,
        P(),
        rows,
        rows,
        P(("x", "z"), None, ("y", "core")),
        P(("x", "z"), None, ("y", "core")),
        P(("x", "z"), ("y", "core"), None),
    )
    return jax.shard_map(body, mesh=fine, in_specs=in_specs, out_specs=(rows, rows), check_vma=False)
```
